512 devices in a mesh: tm: 64 (over z, y), chan: 8 (over x, core).
Axes of the slice: x: 4, y: 8, z: 8, core: 2. Of those that a mesh axis runs over, the one named last changes fastest.
Arguments:
- values: bfloat16 [16384, 4096], P('tm', 'chan'), may hold values from -6 to 6
- gates: bfloat16 [16384, 4096], P('tm', 'chan'), may hold values from -6 to 6
- cotangent: bfloat16 [16384, 4096], P('tm', 'chan'), may hold values from -6 to 6
- kernel_taps: bfloat16 [256, 4096], P(None, 'chan'), may hold values from -0.375 to 0.375
- value_weight: bfloat16 [4096, 4096], P('tm', 'chan'), may hold values from -0.09375 to 0.09375
- gate_weight: bfloat16 [4096, 4096], P('tm', 'chan'), may hold values from -0.09375 to 0.09375
Outputs:
- grad_input: bfloat16 [16384, 4096], P('tm', 'chan')
- kernel_grad: float32 [256, 4096], P('tm', 'chan')
The draws below stay inside these ranges and needn't reach their ends.
All inputs are finite; a program needn't handle non-finite values.
Results may differ from the reference program's by a relative error of at most 0.017.
Values may be sent and summed in bfloat16 or wider, within the bound.
A program may use at most 64 MiB of HBM per device.

```python
import math
import jax
import jax.numpy as jnp
from jax import lax

D = 4096
KLEN = 256
TOKENS = 16384
N_CHAN = 8


def block_levels(stream_key, extent, shards, low, high):
    factor_of, own = 1.0, jax.random.fold_in(stream_key, 6)
    for axis_at, shards_of in shards:
        steps = jnp.exp(jax.random.uniform(jax.random.fold_in(own, axis_at), (shards_of,), jnp.float32, low / len(shards), high / len(shards)))
        factor_of = factor_of * jnp.repeat(steps, extent[axis_at] // shards_of).reshape([-1 if axis == axis_at else 1 for axis in range(len(extent))])
    return factor_of


def scatter_about(stream_key, extent, width, bound, cuts=(), kind=jnp.bfloat16):
    loudness = block_levels(stream_key, extent, cuts, -0.22, 0.18) if cuts else 1.0
    entries = jax.random.normal(stream_key, extent, jnp.float32) * width * loudness
    return jnp.minimum(jnp.maximum(entries, -bound), bound).astype(kind)


def setup_inputs(seed: int = 0) -> dict:
    seeds = jax.random.split(jax.random.key(seed), 7)
    values = scatter_about(seeds[0], (TOKENS, D), 1.0, 6.0, ((0, 64), (1, 8)))
    gates = scatter_about(seeds[1], (TOKENS, D), 1.0, 6.0, ((0, 64), (1, 8)))
    cotangent = scatter_about(seeds[2], (TOKENS, D), 1.0, 6.0, ((0, 64), (1, 8)))
    kernel_taps = scatter_about(seeds[3], (KLEN, D), KLEN ** -0.5, 0.375, ((1, 8),))
    value_weight = scatter_about(seeds[4], (D, D), D ** -0.5, 0.09375, ((0, 64), (1, 8)))
    gate_weight = scatter_about(seeds[5], (D, D), D ** -0.5, 0.09375, ((0, 64), (1, 8)))
    return dict(values=values, gates=gates, cotangent=cotangent, kernel_taps=kernel_taps, value_weight=value_weight, gate_weight=gate_weight)


def reference(values, gates, cotangent, kernel_taps, value_weight, gate_weight):
    step_count = values.shape[0]
    feature_count = values.shape[1]
    fft_len = step_count + KLEN
    group_size = feature_count // N_CHAN
    norm_scale = 1.0 / math.sqrt(step_count)
    input_sum = jnp.zeros((step_count, feature_count), jnp.float32)
    kernel_columns = []
    for group_index in range(N_CHAN):
        low_col = group_index * group_size
        high_col = low_col + group_size
        value_f = values[:, low_col:high_col].astype(jnp.float32)
        gate_f = gates[:, low_col:high_col].astype(jnp.float32)
        cot_f = cotangent[:, low_col:high_col].astype(jnp.float32)
        taps_f = kernel_taps[:, low_col:high_col].astype(jnp.float32)
        value_freq = jnp.fft.rfft(value_f, n=fft_len, axis=0)
        taps_freq = jnp.fft.rfft(taps_f, n=fft_len, axis=0)
        conv_out = jnp.fft.irfft(value_freq * taps_freq, n=fft_len, axis=0)[:step_count]
        grad_conv = (cot_f * gate_f).astype(jnp.bfloat16)
        grad_gate = (cot_f * conv_out).astype(jnp.bfloat16)
        grad_freq = jnp.fft.rfft(grad_conv.astype(jnp.float32), n=fft_len, axis=0)
        grad_value = jnp.fft.irfft(grad_freq * jnp.conj(taps_freq), n=fft_len, axis=0)[:step_count].astype(jnp.bfloat16)
        kernel_part = jnp.fft.irfft(grad_freq * jnp.conj(value_freq), n=fft_len, axis=0)[:KLEN] * norm_scale
        kernel_columns.append(kernel_part.astype(jnp.float32))
        partial_sum = jnp.dot(grad_value, value_weight[:, low_col:high_col].T, preferred_element_type=jnp.float32)
        partial_sum = partial_sum + jnp.dot(grad_gate, gate_weight[:, low_col:high_col].T, preferred_element_type=jnp.float32)
        rounded = lax.optimization_barrier(partial_sum.astype(jnp.bfloat16))
        input_sum = input_sum + rounded.astype(jnp.float32)
    kernel_grad = jnp.concatenate(kernel_columns, axis=1).astype(jnp.float32)
    return (input_sum.astype(jnp.bfloat16), kernel_grad)
```

```python
import functools
import math

import jax
import jax.numpy as jnp
import ml_dtypes
import numpy as np
from jax import lax
from jax.experimental import pallas as pl
from jax.experimental.pallas import tpu as pltpu
from jax.sharding import PartitionSpec as P

MESH = pl.DeviceIdType.MESH
BF16 = jnp.bfloat16
F32 = jnp.float32
RING = 8
SLOT = {0: 0, -1: 1, 1: 2, -2: 3, 2: 4, -3: 5, 3: 6, 4: 7}


def split_table(table):
    high = table.astype(ml_dtypes.bfloat16)
    low = (table - high.astype(np.float64)).astype(ml_dtypes.bfloat16)
    return jnp.asarray(high), jnp.asarray(low)


def dft_tables(half):
    length = 2 * half
    step = np.arange(length)
    freq = np.arange(half)
    angle = (freq[:, None] * step[None, :] % length) * (2.0 * np.pi / length)
    cosine, sine = np.cos(angle), -np.sin(angle)
    sine[0] = np.where(step % 2 == 0, 1.0, -1.0)
    forward = np.concatenate([cosine, sine], 0)
    weight = np.full((length,), 2.0 / length)
    weight[0] = weight[half] = 1.0 / length
    inverse = (forward[:, :half] * weight[:, None]).T
    return forward, inverse


def wrap(index):
    return lax.rem(index + RING, RING)


def slot_of(distance):
    far = lax.div(distance, 4)
    return (1 - far) * 2 * distance + far * (15 - 2 * distance)


def mm(left, right):
    return jnp.dot(left, right, preferred_element_type=F32)


def kernel(
    norm_scale,
    values,
    gates,
    cotangent,
    taps,
    value_weight,
    gate_weight,
    fwd_hi,
    fwd_lo,
    inv_hi,
    inv_lo,
    out,
    kernel_grad,
    gather_a,
    gather_b,
    value_rim,
    grad_win,
    spec_v,
    spec_g,
    spec_p,
    spec_t,
    prod_hi,
    prod_lo,
    left_v,
    left_g,
    part_a,
    part_b,
    got_a,
    got_b,
    kz_send,
    kz_got,
    ky_send,
    ky_got,
    rim_send_sem,
    rim_recv_sem,
    p1_send,
    p1_recv,
    p2_send,
    p2_recv,
    a_send,
    a_recv,
    b_send,
    b_recv,
    kz_send_sem,
    kz_recv_sem,
    ky_send_sem,
    ky_recv_sem,
):
    rows = values.shape[0]
    tm = lax.axis_index("tm")
    me = lax.axis_index("chan")
    z, y = lax.div(tm, RING), lax.rem(tm, RING)

    def at_y(distance):
        return z * RING + wrap(y + distance)

    def at_z(distance):
        return wrap(z + distance) * RING + y

    def remote(src, dst, send_sem, recv_sem, axis, index):
        return pltpu.make_async_remote_copy(
            src_ref=src,
            dst_ref=dst,
            send_sem=send_sem,
            recv_sem=recv_sem,
            device_id={axis: index},
            device_id_type=MESH,
        )

    barrier = pltpu.get_barrier_semaphore()

    def greet(axis, index):
        pl.semaphore_signal(barrier, inc=1, device_id={axis: index}, device_id_type=MESH)

    for distance in range(1, RING):
        greet("tm", at_y(distance))
        greet("tm", at_z(distance))
        greet("chan", wrap(me + distance))
    after = lax.rem(tm + 1, RING * RING)
    before = lax.rem(tm + RING * RING - 1, RING * RING)
    greet("tm", after)
    greet("tm", before)

    half = value_weight.shape[0] // 2
    for which, weight in ((0, value_weight), (1, gate_weight)):
        gather_a[0, 0, which] = weight[:half]
        gather_b[0, 0, which] = weight[half:]
    grad_win[:rows] = (cotangent[...].astype(F32) * gates[...].astype(F32)).astype(BF16)

    pl.semaphore_wait(barrier, 3 * (RING - 1) + 2)

    sends = []

    def go(copy):
        copy.start()
        sends.append(copy)
        return copy

    rim_v = go(remote(values, value_rim, rim_send_sem.at[0], rim_recv_sem.at[0], "tm", after))
    rim_g = go(
        remote(
            grad_win.at[:rows], grad_win.at[rows:], rim_send_sem.at[1], rim_recv_sem.at[1], "tm", before
        )
    )

    buffers = (gather_a, gather_b)
    first_axis = (at_y, at_z)
    second_axis = (at_z, at_y)
    stage1, stage2 = {}, {}

    def send1(color, way, distance):
        sign = -1 if way == 0 else 1
        src = buffers[color].at[0, SLOT[sign * distance]]
        if distance < 3:
            dst = buffers[color].at[0, SLOT[sign * (distance + 1)]]
        else:
            src, dst = src.at[way], buffers[color].at[0, SLOT[4], way]
        stage1[color, way, distance] = go(
            remote(
                src,
                dst,
                p1_send.at[color, way, distance],
                p1_recv.at[color, way, distance],
                "tm",
                first_axis[color](-sign),
            )
        )

    def send2(color, way, distance, part):
        sign = -1 if way == 0 else 1
        blocks = pl.ds(4 * part, 4)
        src = buffers[color].at[SLOT[sign * distance], blocks]
        target = SLOT[4] if distance == 3 else SLOT[sign * (distance + 1)]
        dst = buffers[color].at[target, blocks]
        at = 6 if distance == 3 else 2 * distance + part
        stage2[color, way, distance, part] = go(
            remote(
                src,
                dst,
                p2_send.at[color, way, at],
                p2_recv.at[color, way, at],
                "tm",
                second_axis[color](-sign),
            )
        )

    pairs = [(color, way) for way in (0, 1) for color in (0, 1)]

    def serve1(distance):
        for color, way in pairs:
            stage1[color, way, distance - 1].wait_recv()
            if distance < 4:
                send1(color, way, distance)

    def start2(part):
        for color, way in pairs:
            send2(color, way, 0, part)

    def serve2(distance, part):
        for color, way in pairs:
            stage2[color, way, distance - 1, part].wait_recv()
            if distance < 3 or part == way:
                send2(color, way, distance, part)

    for color, way in pairs:
        send1(color, way, 0)

    def forward(first, data):
        cols = slice(0, rows) if first else slice(rows, 2 * rows)
        return mm(fwd_hi[:, cols], data) + mm(fwd_lo[:, cols], data)

    spec_t[...] = forward(True, taps[...])
    serve1(1)
    spec_p[...] = forward(True, grad_win[:rows])
    serve1(2)
    start2(0)
    spec_v[...] = forward(False, values[...])
    serve1(3)
    rim_v.wait_recv()
    has_before = (tm > 0).astype(F32)
    spec_v[...] = spec_v[...] + forward(True, value_rim[...]) * has_before
    rim_g.wait_recv()
    has_after = (tm < RING * RING - 1).astype(F32)
    spec_g[...] = spec_p[...] + forward(False, grad_win[rows:]) * has_after
    serve1(4)
    start2(1)

    chans = values.shape[1]
    width = 128
    row_at = lax.broadcasted_iota(jnp.int32, (rows, width), 0)
    first_row = row_at == 0
    sign = (1 - 2 * (row_at & 1)).astype(F32)

    def product(left_re, left_im, right_re, right_im, flip):
        cross = left_im * right_im
        real = left_re * right_re
        if flip:
            imag = left_im * right_re - left_re * right_im
            real = real + jnp.where(first_row, 0.0, cross)
        else:
            imag = left_im * right_re + left_re * right_im
            real = real - jnp.where(first_row, 0.0, cross)
        return real, jnp.where(first_row, cross, imag)

    def keep(real, imag, at):
        for part, data in ((slice(0, rows), real), (slice(rows, 2 * rows), imag)):
            high = data.astype(BF16)
            prod_hi[part, at : at + width] = high
            prod_lo[part, at : at + width] = (data - high.astype(F32)).astype(BF16)

    for col in range(0, chans, width):
        cut = slice(col, col + width)
        v_re, v_im = spec_v[:rows, cut], spec_v[rows:, cut]
        t_re, t_im = spec_t[:rows, cut], spec_t[rows:, cut]
        g_re, g_im = spec_g[:rows, cut], spec_g[rows:, cut]
        p_re, p_im = spec_p[:rows, cut] * sign, spec_p[rows:, cut] * sign
        real, imag = product(v_re, v_im, t_re, t_im, False)
        keep(real * sign, imag * sign, col)
        real, imag = product(g_re, g_im, t_re, t_im, True)
        keep(real, imag, chans + col)
        real, imag = product(p_re, p_im, v_re, v_im, True)
        keep(real, imag, 2 * chans + col)

    def backward(index):
        cut = slice(index * chans, (index + 1) * chans)
        return (
            mm(inv_hi[...], prod_hi[:, cut])
            + mm(inv_hi[...], prod_lo[:, cut])
            + mm(inv_lo[...], prod_hi[:, cut])
        )

    partial_kernel = backward(2) * norm_scale
    kz_send[...] = partial_kernel.reshape(kz_send.shape).astype(BF16)
    kz = []
    for distance in range(1, RING):
        kz.append(
            go(
                remote(
                    kz_send.at[wrap(z + distance)],
                    kz_got.at[RING - distance],
                    kz_send_sem.at[RING - distance],
                    kz_recv_sem.at[RING - distance],
                    "tm",
                    at_z(distance),
                )
            )
        )
    serve2(1, 0)
    left_v[...] = backward(1).T.astype(BF16)
    left_g[...] = (cotangent[...].astype(F32) * backward(0)).T.astype(BF16)

    def multiply(color, slots, blocks):
        ref = buffers[color]
        count = (slots[1] - slots[0]) * (blocks[1] - blocks[0]) * half
        total = mm(
            ref[slots[0] : slots[1], blocks[0] : blocks[1], 0].reshape(count, chans), left_v[...]
        )
        total = total + mm(
            ref[slots[0] : slots[1], blocks[0] : blocks[1], 1].reshape(count, chans), left_g[...]
        )
        total = total.astype(BF16)
        for slot in range(slots[0], slots[1]):
            for block in range(blocks[0], blocks[1]):
                at = ((slot - slots[0]) * (blocks[1] - blocks[0]) + block - blocks[0]) * half
                if color == 0:
                    part_a[slot, block] = total[at : at + half]
                else:
                    part_b[block, slot] = total[at : at + half]

    places = {slot: place for place, slot in SLOT.items()}

    def copy_a(slot, part):
        owner = wrap(z + places[slot])
        blocks = pl.ds(4 * part, 4)
        at = wrap(me - owner)
        return owner, remote(
            part_a.at[slot, blocks],
            got_a.at[at, blocks],
            a_send.at[slot, part],
            a_recv.at[at, part],
            "chan",
            owner,
        )

    sent_a = []

    def give_a(slot, part):
        owner, copy = copy_a(slot, part)
        sent_a.append((slot, part))

        @pl.when(owner != me)
        def _():
            copy.start()

    def give_b(group, slots):
        for distance in range(1, RING):
            owner = wrap(me + distance)
            row = slot_of(wrap(owner - z))
            go(
                remote(
                    part_b.at[row, slots],
                    got_b.at[RING - distance, slots],
                    b_send.at[group, RING - distance],
                    b_recv.at[group, RING - distance],
                    "chan",
                    owner,
                )
            )

    multiply(0, (0, 1), (0, 8))
    give_a(0, 0)
    give_a(0, 1)
    multiply(1, (0, 1), (0, 8))
    give_b(0, pl.ds(0, 1))

    ky = []
    for distance in (1, 2, 3):
        slots = (2 * distance - 1, 2 * distance + 1)
        for part in (0, 1):
            if (distance, part) != (1, 0):
                serve2(distance, part)
            for color in (0, 1):
                multiply(color, slots, (4 * part, 4 * part + 4))
                if color == 0:
                    give_a(slots[0], part)
                    give_a(slots[0] + 1, part)
        give_b(distance, pl.ds(slots[0], 2))
        if distance == 1:
            for copy in kz:
                copy.wait_recv()
            total = kz_send[z].astype(F32)
            for index in range(1, RING):
                total = total + kz_got[index].astype(F32)
            lags = ky_send.shape[1]
            for index in range(RING):
                ky_send[index] = total[index * lags : (index + 1) * lags]
            for index in range(1, RING):
                ky.append(
                    go(
                        remote(
                            ky_send.at[wrap(y + index)],
                            ky_got.at[RING - index],
                            ky_send_sem.at[RING - index],
                            ky_recv_sem.at[RING - index],
                            "tm",
                            at_y(index),
                        )
                    )
                )
        if distance == 2:
            for copy in ky:
                copy.wait_recv()
            total = ky_send[y]
            for index in range(1, RING):
                total = total + ky_got[index]
            kernel_grad[...] = total

    for color, way in pairs:
        stage2[color, way, 3, way].wait_recv()
    multiply(0, (7, 8), (0, 8))
    give_a(7, 0)
    give_a(7, 1)
    multiply(1, (7, 8), (0, 8))
    give_b(4, pl.ds(7, 1))

    for index in range(1, RING):
        for part in (0, 1):
            blocks = pl.ds(4 * part, 4)
            remote(
                part_a.at[0, blocks],
                got_a.at[index, blocks],
                a_send.at[0, part],
                a_recv.at[index, part],
                "chan",
                wrap(me + index),
            ).wait_recv()
        for group in range(5):
            slots = pl.ds(0, 1) if group == 0 else pl.ds(2 * group - 1, 1 if group == 4 else 2)
            remote(
                part_b.at[0, slots],
                got_b.at[index, slots],
                b_send.at[group, index],
                b_recv.at[group, index],
                "chan",
                wrap(me + index),
            ).wait_recv()

    own = slot_of(wrap(me - z))
    for pair in range(RING // 2):
        pieces = []
        for place in (2 * pair, 2 * pair + 1):
            block = slot_of(wrap(place - y))
            for part, got in ((part_a, got_a), (part_b, got_b)):
                total = part[own, block].astype(F32)
                for index in range(1, RING):
                    total = total + got[index, block].astype(F32)
                pieces.append(total)
        merged = jnp.concatenate(pieces, 0)
        out[:, 4 * half * pair : 4 * half * (pair + 1)] = merged.T.astype(BF16)

    for copy in sends:
        copy.wait_send()
    for slot, part in sent_a:
        owner, copy = copy_a(slot, part)

        @pl.when(owner != me)
        def _():
            copy.wait_send()


def body(norm_scale, tables, *args):
    values, _, _, taps, value_weight, _ = args
    rows, chans = values.shape
    half = value_weight.shape[0] // 2
    lags = taps.shape[0] // (RING * RING)
    assert taps.shape[0] == rows and lax.axis_size("tm") == RING * RING
    assert lax.axis_size("chan") == RING and chans == RING * 2 * half
    vmem = pl.BlockSpec(memory_space=pltpu.VMEM)
    dma = pltpu.SemaphoreType.DMA
    return pl.pallas_call(
        functools.partial(kernel, norm_scale),
        out_shape=(
            jax.ShapeDtypeStruct((rows, chans), BF16),
            jax.ShapeDtypeStruct((lags, chans), F32),
        ),
        in_specs=[vmem] * 10,
        out_specs=(vmem, vmem),
        scratch_shapes=[
            pltpu.VMEM((RING, RING, 2, half, chans), BF16),
            pltpu.VMEM((RING, RING, 2, half, chans), BF16),
            pltpu.VMEM((rows, chans), BF16),
            pltpu.VMEM((2 * rows, chans), BF16),
            pltpu.VMEM((2 * rows, chans), F32),
            pltpu.VMEM((2 * rows, chans), F32),
            pltpu.VMEM((2 * rows, chans), F32),
            pltpu.VMEM((2 * rows, chans), F32),
            pltpu.VMEM((2 * rows, 3 * chans), BF16),
            pltpu.VMEM((2 * rows, 3 * chans), BF16),
            pltpu.VMEM((chans, rows), BF16),
            pltpu.VMEM((chans, rows), BF16),
            pltpu.VMEM((RING, RING, half, rows), BF16),
            pltpu.VMEM((RING, RING, half, rows), BF16),
            pltpu.VMEM((RING, RING, half, rows), BF16),
            pltpu.VMEM((RING, RING, half, rows), BF16),
            pltpu.VMEM((RING, RING * lags, chans), BF16),
            pltpu.VMEM((RING, RING * lags, chans), BF16),
            pltpu.VMEM((RING, lags, chans), F32),
            pltpu.VMEM((RING, lags, chans), F32),
            dma((2,)),
            dma((2,)),
            dma((2, 2, 4)),
            dma((2, 2, 4)),
            dma((2, 2, 7)),
            dma((2, 2, 7)),
            dma((RING, 2)),
            dma((RING, 2)),
            dma((5, RING)),
            dma((5, RING)),
            dma((RING,)),
            dma((RING,)),
            dma((RING,)),
            dma((RING,)),
        ],
        compiler_params=pltpu.CompilerParams(
            collective_id=0, has_side_effects=True, vmem_limit_bytes=56 * 1024 * 1024
        ),
    )(*args, *tables)


def solution(mesh):
    placed = (
        P("tm", "chan"),
        P("tm", "chan"),
        P("tm", "chan"),
        P(None, "chan"),
        P("tm", "chan"),
        P("tm", "chan"),
    )

    def program(values, gates, cotangent, kernel_taps, value_weight, gate_weight):
        fwd, inv = dft_tables(kernel_taps.shape[0])
        tables = (*split_table(fwd), *split_table(inv))
        norm_scale = 1.0 / math.sqrt(values.shape[0])
        return jax.shard_map(
            lambda *args: body(norm_scale, args[6:], *args[:6]),
            mesh=mesh,
            in_specs=placed + (P(),) * 4,
            out_specs=(P("tm", "chan"), P("tm", "chan")),
            check_vma=False,
        )(values, gates, cotangent, kernel_taps, value_weight, gate_weight, *tables)

    return program
```

```python
import functools
import math

import jax
import jax.numpy as jnp
import ml_dtypes
import numpy as np
from jax import lax
from jax.experimental import pallas as pl
from jax.experimental.pallas import tpu as pltpu
from jax.sharding import PartitionSpec as P

MESH = pl.DeviceIdType.MESH
BF16 = jnp.bfloat16
F32 = jnp.float32
RING = 8
SLOT = {0: 0, -1: 1, 1: 2, -2: 3, 2: 4, -3: 5, 3: 6, 4: 7}
GROUPS = ((0, 1), (1, 3), (3, 5), (5, 7), (7, 8))
PARTS = ((0, 5), (5, 8))
UNITS = [(color, slots, blocks) for slots in GROUPS for blocks in PARTS for color in (0, 1)]


def arrivals():
    found = []
    for way in (0, 1):
        for color in (0, 1):
            found += [(1, color, way, distance, 0) for distance in range(1, 5)]
            for distance in range(1, 5):
                for group, (low, high) in enumerate(GROUPS):
                    if distance < 4 or max(low, 4 * way) < min(high, 4 * way + 4):
                        found.append((2, color, way, distance, group))
    return sorted(found, key=lambda event: (event[3] + event[4], event[0], event[3]))


EVENTS = arrivals()
CHORE_EVERY = 7


def split_table(table):
    high = table.astype(ml_dtypes.bfloat16)
    low = (table - high.astype(np.float64)).astype(ml_dtypes.bfloat16)
    return jnp.asarray(high), jnp.asarray(low)


def dft_tables(half):
    length = 2 * half
    step = np.arange(length)
    freq = np.arange(half)
    angle = (freq[:, None] * step[None, :] % length) * (2.0 * np.pi / length)
    cosine, sine = np.cos(angle), -np.sin(angle)
    sine[0] = np.where(step % 2 == 0, 1.0, -1.0)
    forward = np.concatenate([cosine, sine], 0)
    weight = np.full((length,), 2.0 / length)
    weight[0] = weight[half] = 1.0 / length
    inverse = (forward[:, :half] * weight[:, None]).T
    return forward, inverse


def wrap(index):
    return lax.rem(index + RING, RING)


def slot_of(distance):
    far = lax.div(distance, 4)
    return (1 - far) * 2 * distance + far * (15 - 2 * distance)


def mm(left, right):
    return jnp.dot(left, right, preferred_element_type=F32)


def kernel(
    norm_scale,
    values_in,
    gates_in,
    cotangent_in,
    taps_in,
    value_weight,
    gate_weight,
    fwd_hi_in,
    fwd_lo_in,
    inv_hi_in,
    inv_lo_in,
    out,
    kernel_grad,
    values,
    gates,
    cotangent,
    taps,
    fwd_hi,
    fwd_lo,
    inv_hi,
    inv_lo,
    gather_a,
    gather_b,
    value_rim,
    grad_win,
    spec_v,
    spec_g,
    spec_p,
    spec_t,
    prod_hi,
    prod_lo,
    left_v,
    left_g,
    part_a,
    part_b,
    sib_a,
    sib_b,
    got_a,
    got_b,
    lag_part,
    kz_send,
    kz_got,
    lag_row,
    ky_send,
    ky_got,
    local_sem,
    rim_send_sem,
    rim_recv_sem,
    p1_send,
    p1_recv,
    p2_send,
    p2_recv,
    sib_send,
    sib_recv,
    a_send,
    a_recv,
    b_send,
    b_recv,
    kz_send_sem,
    kz_recv_sem,
    ky_send_sem,
    ky_recv_sem,
):
    rows = values.shape[0]
    tm = lax.axis_index("tm")
    me = lax.axis_index("chan")
    z, y = lax.div(tm, RING), lax.rem(tm, RING)

    def at_y(distance):
        return z * RING + wrap(y + distance)

    def at_z(distance):
        return wrap(z + distance) * RING + y

    def remote(src, dst, send_sem, recv_sem, axis, index):
        return pltpu.make_async_remote_copy(
            src_ref=src,
            dst_ref=dst,
            send_sem=send_sem,
            recv_sem=recv_sem,
            device_id={axis: index},
            device_id_type=MESH,
        )

    barrier = pltpu.get_barrier_semaphore()

    def greet(axis, index):
        pl.semaphore_signal(barrier, inc=1, device_id={axis: index}, device_id_type=MESH)

    half = value_weight.shape[0] // 2
    loads = []

    def load(src, dst):
        copy = pltpu.make_async_copy(src, dst, local_sem.at[len(loads)])
        copy.start()
        loads.append(copy)
        return copy

    own_rows = [
        load(weight.at[pl.ds(half * color, half)], gather.at[0, 0, which])
        for color, gather in ((0, gather_a), (1, gather_b))
        for which, weight in ((0, value_weight), (1, gate_weight))
    ]
    for distance in range(1, RING):
        greet("chan", wrap(me + distance))
    for distance in (-1, 1):
        greet("tm", at_y(distance))
        greet("tm", at_z(distance))
    after = lax.rem(tm + 1, RING * RING)
    before = lax.rem(tm + RING * RING - 1, RING * RING)
    greet("tm", after)
    greet("tm", before)
    streams = [load(cotangent_in, cotangent), load(gates_in, gates), load(values_in, values)]
    ahead = [load(taps_in, taps), load(fwd_hi_in, fwd_hi), load(fwd_lo_in, fwd_lo)]
    later = [load(inv_hi_in, inv_hi), load(inv_lo_in, inv_lo)]

    pl.semaphore_wait(barrier, (RING - 1) + 6)
    for copy in own_rows:
        copy.wait()

    sends = []

    def go(copy):
        copy.start()
        sends.append(copy)
        return copy

    buffers = (gather_a, gather_b)
    first_axis = (at_y, at_z)
    second_axis = (at_z, at_y)
    flights = {}

    def send1(color, way, distance):
        sign = -1 if way == 0 else 1
        src = buffers[color].at[0, SLOT[sign * distance]]
        if distance < 3:
            dst = buffers[color].at[0, SLOT[sign * (distance + 1)]]
        else:
            src, dst = src.at[way], buffers[color].at[0, SLOT[4], way]
        flights[1, color, way, distance + 1, 0] = go(
            remote(
                src,
                dst,
                p1_send.at[color, way, distance],
                p1_recv.at[color, way, distance],
                "tm",
                first_axis[color](-sign),
            )
        )

    def send2(color, way, distance, group):
        sign = -1 if way == 0 else 1
        low, high = GROUPS[group]
        target, at = SLOT[4], 15 + group
        if distance < 3:
            target, at = SLOT[sign * (distance + 1)], 5 * distance + group
        else:
            low, high = max(low, 4 * way), min(high, 4 * way + 4)
            if low >= high:
                return
        blocks = pl.ds(low, high - low)
        flights[2, color, way, distance + 1, group] = go(
            remote(
                buffers[color].at[SLOT[sign * distance], blocks],
                buffers[color].at[target, blocks],
                p2_send.at[color, way, at],
                p2_recv.at[color, way, at],
                "tm",
                second_axis[color](-sign),
            )
        )

    pairs = [(color, way) for way in (0, 1) for color in (0, 1)]

    def serve(event):
        stage, color, way, distance, group = event
        flights[event].wait_recv()
        if stage == 1:
            if distance < 4:
                send1(color, way, distance)
            if way == 1:
                for out_way in (0, 1):
                    send2(color, out_way, 0, distance)
        elif distance < 4:
            send2(color, way, distance, group)

    for color, way in pairs:
        send1(color, way, 0)
        send2(color, way, 0, 0)

    for copy in streams:
        copy.wait()
    grad_win[:rows] = (cotangent[...].astype(F32) * gates[...].astype(F32)).astype(BF16)
    rim_v = go(remote(values, value_rim, rim_send_sem.at[0], rim_recv_sem.at[0], "tm", after))
    rim_g = go(
        remote(
            grad_win.at[:rows], grad_win.at[rows:], rim_send_sem.at[1], rim_recv_sem.at[1], "tm", before
        )
    )

    def forward(first, data):
        cols = slice(0, rows) if first else slice(rows, 2 * rows)
        return mm(fwd_hi[:, cols], data) + mm(fwd_lo[:, cols], data)

    steps = {}
    for event in EVENTS:
        steps.setdefault(event[3] + event[4], []).append(event)

    for copy in ahead:
        copy.wait()
    spec_t[...] = forward(True, taps[...])
    spec_p[...] = forward(True, grad_win[:rows])
    for event in steps[1]:
        serve(event)
    spec_v[...] = forward(False, values[...])
    for event in steps[2]:
        serve(event)
    rim_v.wait_recv()
    has_before = (tm > 0).astype(F32)
    spec_v[...] = spec_v[...] + forward(True, value_rim[...]) * has_before
    rim_g.wait_recv()
    has_after = (tm < RING * RING - 1).astype(F32)
    spec_g[...] = spec_p[...] + forward(False, grad_win[rows:]) * has_after

    chans = values.shape[1]
    width = 128
    row_at = lax.broadcasted_iota(jnp.int32, (rows, width), 0)
    first_row = row_at == 0
    sign = (1 - 2 * (row_at & 1)).astype(F32)

    def product(left_re, left_im, right_re, right_im, flip):
        cross = left_im * right_im
        real = left_re * right_re
        if flip:
            imag = left_im * right_re - left_re * right_im
            real = real + jnp.where(first_row, 0.0, cross)
        else:
            imag = left_im * right_re + left_re * right_im
            real = real - jnp.where(first_row, 0.0, cross)
        return real, jnp.where(first_row, cross, imag)

    def keep(real, imag, at):
        for part, data in ((slice(0, rows), real), (slice(rows, 2 * rows), imag)):
            high = data.astype(BF16)
            prod_hi[part, at : at + width] = high
            prod_lo[part, at : at + width] = (data - high.astype(F32)).astype(BF16)

    for col in range(0, chans, width):
        cut = slice(col, col + width)
        v_re, v_im = spec_v[:rows, cut], spec_v[rows:, cut]
        t_re, t_im = spec_t[:rows, cut], spec_t[rows:, cut]
        g_re, g_im = spec_g[:rows, cut], spec_g[rows:, cut]
        p_re, p_im = spec_p[:rows, cut] * sign, spec_p[rows:, cut] * sign
        real, imag = product(v_re, v_im, t_re, t_im, False)
        keep(real * sign, imag * sign, col)
        real, imag = product(g_re, g_im, t_re, t_im, True)
        keep(real, imag, chans + col)
        real, imag = product(p_re, p_im, v_re, v_im, True)
        keep(real, imag, 2 * chans + col)

    def backward(index):
        cut = slice(index * chans, (index + 1) * chans)
        return (
            mm(inv_hi[...], prod_hi[:, cut])
            + mm(inv_hi[...], prod_lo[:, cut])
            + mm(inv_lo[...], prod_hi[:, cut])
        )

    def chain(own, send, got, send_sem, recv_sem, place, to):
        flying = {}

        def step(index):
            arrived = []
            for way, (length, sign) in enumerate(((3, 1), (4, -1))):
                if index > length:
                    continue
                if index:
                    flying[way, index - 1].wait_recv()
                    data = got[way, index - 1].astype(F32)
                if index == length:
                    flying[way] = data
                    continue
                mine = own[wrap(place + sign * (length - index))]
                if index:
                    mine = mine + data
                send[way, index] = mine.astype(send.dtype)
                flying[way, index] = go(
                    remote(
                        send.at[way, index],
                        got.at[way, index],
                        send_sem.at[way, index],
                        recv_sem.at[way, index],
                        "tm",
                        to(sign),
                    )
                )
            if index == 4:
                return own[place] + flying[0] + flying[1]

        return step

    for copy in later:
        copy.wait()
    lag_part[...] = (backward(2) * norm_scale).reshape(lag_part.shape)
    along_z = chain(lag_part, kz_send, kz_got, kz_send_sem, kz_recv_sem, z, at_z)
    along_y = chain(lag_row, ky_send, ky_got, ky_send_sem, ky_recv_sem, y, at_y)
    along_z(0)

    def chore(index):
        if index < 4:
            along_z(index)
        elif index == 4:
            total = along_z(4)
            lags = lag_row.shape[1]
            for at in range(RING):
                lag_row[at] = total[at * lags : (at + 1) * lags]
            along_y(0)
        elif index < 8:
            along_y(index - 4)
        else:
            kernel_grad[...] = along_y(4)

    left_v[...] = backward(1).T.astype(BF16)
    left_g[...] = (cotangent[...].astype(F32) * backward(0)).T.astype(BF16)

    parts = (part_a, part_b)
    pairs_got = (sib_a, sib_b)
    core = lax.rem(me, 2)
    chip = lax.div(me, 2)
    sibling = me + 1 - 2 * core

    def multiply(unit):
        color, slots, blocks = unit
        ref = buffers[color]
        shape = (slots[1] - slots[0], blocks[1] - blocks[0], 2, half // 2, rows)
        count = shape[0] * shape[1] * half
        cut = (slice(*slots), slice(*blocks))
        total = mm(ref[(*cut, 0)].reshape(count, chans), left_v[...])
        total = total + mm(ref[(*cut, 1)].reshape(count, chans), left_g[...])
        parts[color][cut] = total.astype(BF16).reshape(shape)
        at = (pl.ds(slots[0], shape[0]), pl.ds(blocks[0], shape[1]))
        index = UNITS.index(unit)
        return go(
            remote(
                parts[color].at[(*at, 1 - core)],
                pairs_got[color].at[at],
                sib_send.at[index],
                sib_recv.at[index],
                "chan",
                sibling,
            )
        )

    places = {slot: place for place, slot in SLOT.items()}

    def deliveries(unit):
        color, slots, blocks = unit
        group = GROUPS.index(slots)
        part = PARTS.index(blocks)
        found = []
        for slot in range(*(slots if color == 0 else blocks)):
            owner = wrap(z + places[slot])
            at = lax.rem(chip - lax.div(owner, 2) + 4, 4)
            if color == 0:
                lines = pl.ds(blocks[0], blocks[1] - blocks[0])
                src = part_a.at[slot, lines, core]
                dst = got_a.at[at, core, lines]
                sems = a_send.at[slot, part], a_recv.at[part, at, core]
            else:
                lines = pl.ds(slots[0], slots[1] - slots[0])
                src = part_b.at[lines, slot, core]
                dst = got_b.at[at, core, lines]
                sems = b_send.at[group, slot], b_recv.at[group, at, core]
            found.append((owner, src, dst, remote(src, dst, *sems, "chan", owner)))
        return found

    def finish(unit, flight):
        color, slots, blocks = unit
        flight.wait_recv()
        cut = (slice(*slots), slice(*blocks))
        total = parts[color][(*cut, core)].astype(F32) + pairs_got[color][cut].astype(F32)
        parts[color][(*cut, core)] = total.astype(BF16)
        for owner, src, dst, copy in deliveries(unit):

            @pl.when(owner != me)
            def _():
                copy.start()

            @pl.when(owner == me)
            def _():
                dst[...] = src[...]

    def needs(unit):
        color, slots, blocks = unit
        found = set()
        for slot in range(*slots):
            for block in range(*blocks):
                if slot == 0:
                    place = places[block]
                    ways = (0, 1) if place == 4 else (0,) if place < 0 else (1,)
                    if place:
                        found |= {(1, color, way, abs(place), 0) for way in ways}
                else:
                    way = (0 if block < 4 else 1) if slot == 7 else (0 if places[slot] < 0 else 1)
                    group = [low <= block < high for low, high in GROUPS].index(True)
                    found.add((2, color, way, abs(places[slot]), group))
        return found

    served = set(steps[1]) | set(steps[2])
    waiting = list(UNITS)
    pending = []

    def work():
        for unit in list(waiting):
            if needs(unit) <= served:
                waiting.remove(unit)
                pending.append((unit, multiply(unit)))
                if len(pending) > 1:
                    finish(*pending.pop(0))

    work()
    rest = [event for event in EVENTS if event not in served]
    for index, event in enumerate(rest):
        serve(event)
        served.add(event)
        work()
        if index % CHORE_EVERY == CHORE_EVERY - 1 and index // CHORE_EVERY < 8:
            chore(index // CHORE_EVERY + 1)
    assert not waiting
    for unit, flight in pending:
        finish(unit, flight)

    for at in range(4):
        for which in (0, 1) if at else (1 - core,):
            for part, (low, high) in enumerate(PARTS):
                lines = pl.ds(low, high - low)
                remote(
                    part_a.at[0, lines, 0],
                    got_a.at[at, which, lines],
                    a_send.at[0, part],
                    a_recv.at[part, at, which],
                    "chan",
                    sibling,
                ).wait_recv()
            for group, (low, high) in enumerate(GROUPS):
                lines = pl.ds(low, high - low)
                remote(
                    part_b.at[lines, 0, 0],
                    got_b.at[at, which, lines],
                    b_send.at[group, 0],
                    b_recv.at[group, at, which],
                    "chan",
                    sibling,
                ).wait_recv()

    for pair in range(RING // 2):
        pieces = []
        for place in (2 * pair, 2 * pair + 1):
            block = slot_of(wrap(place - y))
            for got in (got_a, got_b):
                for which in (0, 1):
                    total = got[0, which, block].astype(F32)
                    for at in range(1, 4):
                        total = total + got[at, which, block].astype(F32)
                    pieces.append(total)
        merged = jnp.concatenate(pieces, 0)
        out[:, 4 * half * pair : 4 * half * (pair + 1)] = merged.T.astype(BF16)

    for copy in sends:
        copy.wait_send()
    for unit in UNITS:
        for owner, src, dst, copy in deliveries(unit):

            @pl.when(owner != me)
            def _():
                copy.wait_send()


def body(norm_scale, tables, *args):
    values, _, _, taps, value_weight, _ = args
    rows, chans = values.shape
    half = value_weight.shape[0] // 2
    lags = taps.shape[0] // (RING * RING)
    assert taps.shape[0] == rows and lax.axis_size("tm") == RING * RING
    assert lax.axis_size("chan") == RING and chans == RING * 2 * half
    vmem = pl.BlockSpec(memory_space=pltpu.VMEM)
    dma = pltpu.SemaphoreType.DMA
    return pl.pallas_call(
        functools.partial(kernel, norm_scale),
        out_shape=(
            jax.ShapeDtypeStruct((rows, chans), BF16),
            jax.ShapeDtypeStruct((lags, chans), F32),
        ),
        in_specs=[pl.BlockSpec(memory_space=pl.ANY)] * 10,
        out_specs=(vmem, vmem),
        scratch_shapes=[
            pltpu.VMEM((rows, chans), BF16),
            pltpu.VMEM((rows, chans), BF16),
            pltpu.VMEM((rows, chans), BF16),
            pltpu.VMEM((rows, chans), BF16),
            *(pltpu.VMEM(table.shape, BF16) for table in tables),
            pltpu.VMEM((RING, RING, 2, half, chans), BF16),
            pltpu.VMEM((RING, RING, 2, half, chans), BF16),
            pltpu.VMEM((rows, chans), BF16),
            pltpu.VMEM((2 * rows, chans), BF16),
            pltpu.VMEM((2 * rows, chans), F32),
            pltpu.VMEM((2 * rows, chans), F32),
            pltpu.VMEM((2 * rows, chans), F32),
            pltpu.VMEM((2 * rows, chans), F32),
            pltpu.VMEM((2 * rows, 3 * chans), BF16),
            pltpu.VMEM((2 * rows, 3 * chans), BF16),
            pltpu.VMEM((chans, rows), BF16),
            pltpu.VMEM((chans, rows), BF16),
            pltpu.VMEM((RING, RING, 2, half // 2, rows), BF16),
            pltpu.VMEM((RING, RING, 2, half // 2, rows), BF16),
            pltpu.VMEM((RING, RING, half // 2, rows), BF16),
            pltpu.VMEM((RING, RING, half // 2, rows), BF16),
            pltpu.VMEM((4, 2, RING, half // 2, rows), BF16),
            pltpu.VMEM((4, 2, RING, half // 2, rows), BF16),
            pltpu.VMEM((RING, RING * lags, chans), F32),
            pltpu.VMEM((2, 4, RING * lags, chans), BF16),
            pltpu.VMEM((2, 4, RING * lags, chans), BF16),
            pltpu.VMEM((RING, lags, chans), F32),
            pltpu.VMEM((2, 4, lags, chans), F32),
            pltpu.VMEM((2, 4, lags, chans), F32),
            dma((12,)),
            dma((2,)),
            dma((2,)),
            dma((2, 2, 4)),
            dma((2, 2, 4)),
            dma((2, 2, 20)),
            dma((2, 2, 20)),
            dma((len(UNITS),)),
            dma((len(UNITS),)),
            dma((RING, len(PARTS))),
            dma((len(PARTS), 4, 2)),
            dma((len(GROUPS), RING)),
            dma((len(GROUPS), 4, 2)),
            dma((2, 4)),
            dma((2, 4)),
            dma((2, 4)),
            dma((2, 4)),
        ],
        compiler_params=pltpu.CompilerParams(
            collective_id=0, has_side_effects=True, vmem_limit_bytes=56 * 1024 * 1024
        ),
    )(*args, *tables)


def solution(mesh):
    placed = (
        P("tm", "chan"),
        P("tm", "chan"),
        P("tm", "chan"),
        P(None, "chan"),
        P("tm", "chan"),
        P("tm", "chan"),
    )

    def program(values, gates, cotangent, kernel_taps, value_weight, gate_weight):
        fwd, inv = dft_tables(kernel_taps.shape[0])
        tables = (*split_table(fwd), *split_table(inv))
        norm_scale = 1.0 / math.sqrt(values.shape[0])
        return jax.shard_map(
            lambda *args: body(norm_scale, args[6:], *args[:6]),
            mesh=mesh,
            in_specs=placed + (P(),) * 4,
            out_specs=(P("tm", "chan"), P("tm", "chan")),
            check_vma=False,
        )(values, gates, cotangent, kernel_taps, value_weight, gate_weight, *tables)

    return program
```

```python
import functools
import math

import jax
import jax.numpy as jnp
import ml_dtypes
import numpy as np
from jax import lax
from jax.experimental import pallas as pl
from jax.experimental.pallas import tpu as pltpu
from jax.sharding import PartitionSpec as P

MESH = pl.DeviceIdType.MESH
BF16 = jnp.bfloat16
F32 = jnp.float32
RING = 8
SLOT = {0: 0, -1: 1, 1: 2, -2: 3, 2: 4, -3: 5, 3: 6, 4: 7}
GROUPS = ((0, 1), (1, 3), (3, 5), (5, 7), (7, 8))
PARTS = ((0, 5), (5, 8))
UNITS = [(color, slots, blocks) for slots in GROUPS for blocks in PARTS for color in (0, 1)]


def arrivals():
    found = []
    for way in (0, 1):
        for color in (0, 1):
            found += [(1, color, way, distance, 0) for distance in range(1, 5)]
            for distance in range(1, 5):
                for group, (low, high) in enumerate(GROUPS):
                    if distance < 4 or max(low, 4 * way) < min(high, 4 * way + 4):
                        found.append((2, color, way, distance, group))
    return sorted(found, key=lambda event: (event[3] + event[4], event[0], event[3]))


EVENTS = arrivals()
CHORES = (8, 20, 32, 44, 52, 60, 64, 68)


def split_table(table):
    high = table.astype(ml_dtypes.bfloat16)
    low = (table - high.astype(np.float64)).astype(ml_dtypes.bfloat16)
    return jnp.asarray(high), jnp.asarray(low)


def dft_tables(half):
    length = 2 * half
    step = np.arange(length)
    freq = np.arange(half)
    angle = (freq[:, None] * step[None, :] % length) * (2.0 * np.pi / length)
    cosine, sine = np.cos(angle), -np.sin(angle)
    sine[0] = np.where(step % 2 == 0, 1.0, -1.0)
    forward = np.concatenate([cosine, sine], 0)
    weight = np.full((length,), 2.0 / length)
    weight[0] = weight[half] = 1.0 / length
    inverse = (forward[:, :half] * weight[:, None]).T
    return forward, inverse


def wrap(index):
    return lax.rem(index + RING, RING)


def slot_of(distance):
    far = lax.div(distance, 4)
    return (1 - far) * 2 * distance + far * (15 - 2 * distance)


def mm(left, right):
    return jnp.dot(left, right, preferred_element_type=F32)


def kernel(
    norm_scale,
    values_in,
    gates_in,
    cotangent_in,
    taps_in,
    value_weight,
    gate_weight,
    fwd_hi_in,
    fwd_lo_in,
    inv_hi_in,
    inv_lo_in,
    out,
    kernel_grad,
    values,
    gates,
    cotangent,
    taps,
    fwd_hi,
    fwd_lo,
    inv_hi,
    inv_lo,
    gather_a,
    gather_b,
    value_rim,
    grad_win,
    spec_v,
    spec_g,
    spec_p,
    spec_t,
    prod_hi,
    prod_lo,
    left_v,
    left_g,
    part_a,
    part_b,
    sib_a,
    sib_b,
    got_a,
    got_b,
    lag_part,
    kz_send,
    kz_got,
    lag_row,
    ky_send,
    ky_got,
    local_sem,
    rim_send_sem,
    rim_recv_sem,
    p1_send,
    p1_recv,
    p2_send,
    p2_recv,
    sib_send,
    sib_recv,
    a_send,
    a_recv,
    b_send,
    b_recv,
    kz_send_sem,
    kz_recv_sem,
    ky_send_sem,
    ky_recv_sem,
):
    rows = values.shape[0]
    tm = lax.axis_index("tm")
    me = lax.axis_index("chan")
    z, y = lax.div(tm, RING), lax.rem(tm, RING)

    def at_y(distance):
        return z * RING + wrap(y + distance)

    def at_z(distance):
        return wrap(z + distance) * RING + y

    def remote(src, dst, send_sem, recv_sem, axis, index):
        return pltpu.make_async_remote_copy(
            src_ref=src,
            dst_ref=dst,
            send_sem=send_sem,
            recv_sem=recv_sem,
            device_id={axis: index},
            device_id_type=MESH,
        )

    barrier = pltpu.get_barrier_semaphore()

    def greet(axis, index):
        pl.semaphore_signal(barrier, inc=1, device_id={axis: index}, device_id_type=MESH)

    half = value_weight.shape[0] // 2
    loads = []

    def load(src, dst):
        copy = pltpu.make_async_copy(src, dst, local_sem.at[len(loads)])
        copy.start()
        loads.append(copy)
        return copy

    own_rows = [
        load(weight.at[pl.ds(half * color, half)], gather.at[0, 0, which])
        for color, gather in ((0, gather_a), (1, gather_b))
        for which, weight in ((0, value_weight), (1, gate_weight))
    ]
    for distance in range(1, RING):
        greet("chan", wrap(me + distance))
    for distance in (-1, 1):
        greet("tm", at_y(distance))
        greet("tm", at_z(distance))
    after = lax.rem(tm + 1, RING * RING)
    before = lax.rem(tm + RING * RING - 1, RING * RING)
    greet("tm", after)
    greet("tm", before)
    streams = [load(cotangent_in, cotangent), load(gates_in, gates), load(values_in, values)]
    ahead = [load(taps_in, taps), load(fwd_hi_in, fwd_hi), load(fwd_lo_in, fwd_lo)]
    later = [load(inv_hi_in, inv_hi), load(inv_lo_in, inv_lo)]

    pl.semaphore_wait(barrier, (RING - 1) + 6)
    for copy in own_rows:
        copy.wait()

    sends = []

    def go(copy):
        copy.start()
        sends.append(copy)
        return copy

    buffers = (gather_a, gather_b)
    first_axis = (at_y, at_z)
    second_axis = (at_z, at_y)
    flights = {}

    def send1(color, way, distance):
        sign = -1 if way == 0 else 1
        src = buffers[color].at[0, SLOT[sign * distance]]
        if distance < 3:
            dst = buffers[color].at[0, SLOT[sign * (distance + 1)]]
        else:
            src, dst = src.at[way], buffers[color].at[0, SLOT[4], way]
        flights[1, color, way, distance + 1, 0] = go(
            remote(
                src,
                dst,
                p1_send.at[color, way, distance],
                p1_recv.at[color, way, distance],
                "tm",
                first_axis[color](-sign),
            )
        )

    def send2(color, way, distance, group):
        sign = -1 if way == 0 else 1
        low, high = GROUPS[group]
        target, at = SLOT[4], 15 + group
        if distance < 3:
            target, at = SLOT[sign * (distance + 1)], 5 * distance + group
        else:
            low, high = max(low, 4 * way), min(high, 4 * way + 4)
            if low >= high:
                return
        blocks = pl.ds(low, high - low)
        flights[2, color, way, distance + 1, group] = go(
            remote(
                buffers[color].at[SLOT[sign * distance], blocks],
                buffers[color].at[target, blocks],
                p2_send.at[color, way, at],
                p2_recv.at[color, way, at],
                "tm",
                second_axis[color](-sign),
            )
        )

    pairs = [(color, way) for way in (0, 1) for color in (0, 1)]

    def serve(event):
        stage, color, way, distance, group = event
        flights[event].wait_recv()
        if stage == 1:
            if distance < 4:
                send1(color, way, distance)
            if way == 1:
                for out_way in (0, 1):
                    send2(color, out_way, 0, distance)
        elif distance < 4:
            send2(color, way, distance, group)

    for color, way in pairs:
        send1(color, way, 0)
        send2(color, way, 0, 0)

    for copy in streams:
        copy.wait()
    grad_win[:rows] = (cotangent[...].astype(F32) * gates[...].astype(F32)).astype(BF16)
    rim_v = go(remote(values, value_rim, rim_send_sem.at[0], rim_recv_sem.at[0], "tm", after))
    rim_g = go(
        remote(
            grad_win.at[:rows], grad_win.at[rows:], rim_send_sem.at[1], rim_recv_sem.at[1], "tm", before
        )
    )

    def forward(first, data):
        cols = slice(0, rows) if first else slice(rows, 2 * rows)
        return mm(fwd_hi[:, cols], data) + mm(fwd_lo[:, cols], data)

    steps = {}
    for event in EVENTS:
        steps.setdefault(event[3] + event[4], []).append(event)

    for copy in ahead:
        copy.wait()
    spec_t[...] = forward(True, taps[...])
    spec_p[...] = forward(True, grad_win[:rows])
    for event in steps[1]:
        serve(event)
    spec_v[...] = forward(False, values[...])
    for event in steps[2]:
        serve(event)
    rim_v.wait_recv()
    has_before = (tm > 0).astype(F32)
    spec_v[...] = spec_v[...] + forward(True, value_rim[...]) * has_before
    rim_g.wait_recv()
    has_after = (tm < RING * RING - 1).astype(F32)
    spec_g[...] = spec_p[...] + forward(False, grad_win[rows:]) * has_after

    chans = values.shape[1]
    width = 128
    row_at = lax.broadcasted_iota(jnp.int32, (rows, width), 0)
    first_row = row_at == 0
    sign = (1 - 2 * (row_at & 1)).astype(F32)

    def product(left_re, left_im, right_re, right_im, flip):
        cross = left_im * right_im
        real = left_re * right_re
        if flip:
            imag = left_im * right_re - left_re * right_im
            real = real + jnp.where(first_row, 0.0, cross)
        else:
            imag = left_im * right_re + left_re * right_im
            real = real - jnp.where(first_row, 0.0, cross)
        return real, jnp.where(first_row, cross, imag)

    def keep(real, imag, at):
        for part, data in ((slice(0, rows), real), (slice(rows, 2 * rows), imag)):
            high = data.astype(BF16)
            prod_hi[part, at : at + width] = high
            prod_lo[part, at : at + width] = (data - high.astype(F32)).astype(BF16)

    for col in range(0, chans, width):
        cut = slice(col, col + width)
        v_re, v_im = spec_v[:rows, cut], spec_v[rows:, cut]
        t_re, t_im = spec_t[:rows, cut], spec_t[rows:, cut]
        g_re, g_im = spec_g[:rows, cut], spec_g[rows:, cut]
        p_re, p_im = spec_p[:rows, cut] * sign, spec_p[rows:, cut] * sign
        real, imag = product(v_re, v_im, t_re, t_im, False)
        keep(real * sign, imag * sign, col)
        real, imag = product(g_re, g_im, t_re, t_im, True)
        keep(real, imag, chans + col)
        real, imag = product(p_re, p_im, v_re, v_im, True)
        keep(real, imag, 2 * chans + col)

    def backward(index):
        cut = slice(index * chans, (index + 1) * chans)
        return (
            mm(inv_hi[...], prod_hi[:, cut])
            + mm(inv_hi[...], prod_lo[:, cut])
            + mm(inv_lo[...], prod_hi[:, cut])
        )

    def chain(own, send, got, send_sem, recv_sem, place, to):
        flying = {}

        def step(index):
            arrived = []
            for way, (length, sign) in enumerate(((3, 1), (4, -1))):
                if index > length:
                    continue
                if index:
                    flying[way, index - 1].wait_recv()
                    data = got[way, index - 1].astype(F32)
                if index == length:
                    flying[way] = data
                    continue
                mine = own[wrap(place + sign * (length - index))]
                if index:
                    mine = mine + data
                send[way, index] = mine.astype(send.dtype)
                flying[way, index] = go(
                    remote(
                        send.at[way, index],
                        got.at[way, index],
                        send_sem.at[way, index],
                        recv_sem.at[way, index],
                        "tm",
                        to(sign),
                    )
                )
            if index == 4:
                return own[place] + flying[0] + flying[1]

        return step

    for copy in later:
        copy.wait()
    lag_part[...] = (backward(2) * norm_scale).reshape(lag_part.shape)
    along_z = chain(lag_part, kz_send, kz_got, kz_send_sem, kz_recv_sem, z, at_z)
    along_y = chain(lag_row, ky_send, ky_got, ky_send_sem, ky_recv_sem, y, at_y)
    along_z(0)

    def chore(index):
        if index < 4:
            along_z(index)
        elif index == 4:
            total = along_z(4)
            lags = lag_row.shape[1]
            for at in range(RING):
                lag_row[at] = total[at * lags : (at + 1) * lags]
            along_y(0)
        elif index < 8:
            along_y(index - 4)
        else:
            kernel_grad[...] = along_y(4)

    left_v[...] = backward(1).T.astype(BF16)
    left_g[...] = (cotangent[...].astype(F32) * backward(0)).T.astype(BF16)

    parts = (part_a, part_b)
    pairs_got = (sib_a, sib_b)
    core = lax.rem(me, 2)
    chip = lax.div(me, 2)
    sibling = me + 1 - 2 * core

    def multiply(unit):
        color, slots, blocks = unit
        ref = buffers[color]
        shape = (slots[1] - slots[0], blocks[1] - blocks[0], 2, half // 2, rows)
        count = shape[0] * shape[1] * half
        cut = (slice(*slots), slice(*blocks))
        total = mm(ref[(*cut, 0)].reshape(count, chans), left_v[...])
        total = total + mm(ref[(*cut, 1)].reshape(count, chans), left_g[...])
        parts[color][cut] = total.astype(BF16).reshape(shape)
        at = (pl.ds(slots[0], shape[0]), pl.ds(blocks[0], shape[1]))
        index = UNITS.index(unit)
        return go(
            remote(
                parts[color].at[(*at, 1 - core)],
                pairs_got[color].at[at],
                sib_send.at[index],
                sib_recv.at[index],
                "chan",
                sibling,
            )
        )

    places = {slot: place for place, slot in SLOT.items()}

    def deliveries(unit):
        color, slots, blocks = unit
        group = GROUPS.index(slots)
        part = PARTS.index(blocks)
        found = []
        for slot in range(*(slots if color == 0 else blocks)):
            owner = wrap(z + places[slot])
            at = lax.rem(chip - lax.div(owner, 2) + 4, 4)
            if color == 0:
                lines = pl.ds(blocks[0], blocks[1] - blocks[0])
                src = part_a.at[slot, lines, core]
                dst = got_a.at[at, core, lines]
                sems = a_send.at[slot, part], a_recv.at[part, at, core]
            else:
                lines = pl.ds(slots[0], slots[1] - slots[0])
                src = part_b.at[lines, slot, core]
                dst = got_b.at[at, core, lines]
                sems = b_send.at[group, slot], b_recv.at[group, at, core]
            found.append((owner, src, dst, remote(src, dst, *sems, "chan", owner)))
        return found

    def finish(unit, flight):
        color, slots, blocks = unit
        flight.wait_recv()
        cut = (slice(*slots), slice(*blocks))
        total = parts[color][(*cut, core)].astype(F32) + pairs_got[color][cut].astype(F32)
        parts[color][(*cut, core)] = total.astype(BF16)
        for owner, src, dst, copy in deliveries(unit):

            @pl.when(owner != me)
            def _():
                copy.start()

            @pl.when(owner == me)
            def _():
                dst[...] = src[...]

    def needs(unit):
        color, slots, blocks = unit
        found = set()
        for slot in range(*slots):
            for block in range(*blocks):
                if slot == 0:
                    place = places[block]
                    ways = (0, 1) if place == 4 else (0,) if place < 0 else (1,)
                    if place:
                        found |= {(1, color, way, abs(place), 0) for way in ways}
                else:
                    way = (0 if block < 4 else 1) if slot == 7 else (0 if places[slot] < 0 else 1)
                    group = [low <= block < high for low, high in GROUPS].index(True)
                    found.add((2, color, way, abs(places[slot]), group))
        return found

    served = set(steps[1]) | set(steps[2])
    waiting = list(UNITS)
    pending = []

    def work():
        for unit in list(waiting):
            if needs(unit) <= served:
                waiting.remove(unit)
                pending.append((unit, multiply(unit)))
                if len(pending) > 1:
                    finish(*pending.pop(0))

    work()
    rest = [event for event in EVENTS if event not in served]
    for index, event in enumerate(rest):
        serve(event)
        served.add(event)
        work()
        if index + 1 in CHORES:
            chore(CHORES.index(index + 1) + 1)
    assert not waiting
    for unit, flight in pending:
        finish(unit, flight)

    for at in range(4):
        for which in (0, 1) if at else (1 - core,):
            for part, (low, high) in enumerate(PARTS):
                lines = pl.ds(low, high - low)
                remote(
                    part_a.at[0, lines, 0],
                    got_a.at[at, which, lines],
                    a_send.at[0, part],
                    a_recv.at[part, at, which],
                    "chan",
                    sibling,
                ).wait_recv()
            for group, (low, high) in enumerate(GROUPS):
                lines = pl.ds(low, high - low)
                remote(
                    part_b.at[lines, 0, 0],
                    got_b.at[at, which, lines],
                    b_send.at[group, 0],
                    b_recv.at[group, at, which],
                    "chan",
                    sibling,
                ).wait_recv()

    for pair in range(RING // 2):
        pieces = []
        for place in (2 * pair, 2 * pair + 1):
            block = slot_of(wrap(place - y))
            for got in (got_a, got_b):
                for which in (0, 1):
                    total = got[0, which, block].astype(F32)
                    for at in range(1, 4):
                        total = total + got[at, which, block].astype(F32)
                    pieces.append(total)
        merged = jnp.concatenate(pieces, 0)
        out[:, 4 * half * pair : 4 * half * (pair + 1)] = merged.T.astype(BF16)

    for copy in sends:
        copy.wait_send()
    for unit in UNITS:
        for owner, src, dst, copy in deliveries(unit):

            @pl.when(owner != me)
            def _():
                copy.wait_send()


def body(norm_scale, tables, *args):
    values, _, _, taps, value_weight, _ = args
    rows, chans = values.shape
    half = value_weight.shape[0] // 2
    lags = taps.shape[0] // (RING * RING)
    assert taps.shape[0] == rows and lax.axis_size("tm") == RING * RING
    assert lax.axis_size("chan") == RING and chans == RING * 2 * half
    vmem = pl.BlockSpec(memory_space=pltpu.VMEM)
    dma = pltpu.SemaphoreType.DMA
    return pl.pallas_call(
        functools.partial(kernel, norm_scale),
        out_shape=(
            jax.ShapeDtypeStruct((rows, chans), BF16),
            jax.ShapeDtypeStruct((lags, chans), F32),
        ),
        in_specs=[pl.BlockSpec(memory_space=pl.ANY)] * 10,
        out_specs=(vmem, vmem),
        scratch_shapes=[
            pltpu.VMEM((rows, chans), BF16),
            pltpu.VMEM((rows, chans), BF16),
            pltpu.VMEM((rows, chans), BF16),
            pltpu.VMEM((rows, chans), BF16),
            *(pltpu.VMEM(table.shape, BF16) for table in tables),
            pltpu.VMEM((RING, RING, 2, half, chans), BF16),
            pltpu.VMEM((RING, RING, 2, half, chans), BF16),
            pltpu.VMEM((rows, chans), BF16),
            pltpu.VMEM((2 * rows, chans), BF16),
            pltpu.VMEM((2 * rows, chans), F32),
            pltpu.VMEM((2 * rows, chans), F32),
            pltpu.VMEM((2 * rows, chans), F32),
            pltpu.VMEM((2 * rows, chans), F32),
            pltpu.VMEM((2 * rows, 3 * chans), BF16),
            pltpu.VMEM((2 * rows, 3 * chans), BF16),
            pltpu.VMEM((chans, rows), BF16),
            pltpu.VMEM((chans, rows), BF16),
            pltpu.VMEM((RING, RING, 2, half // 2, rows), BF16),
            pltpu.VMEM((RING, RING, 2, half // 2, rows), BF16),
            pltpu.VMEM((RING, RING, half // 2, rows), BF16),
            pltpu.VMEM((RING, RING, half // 2, rows), BF16),
            pltpu.VMEM((4, 2, RING, half // 2, rows), BF16),
            pltpu.VMEM((4, 2, RING, half // 2, rows), BF16),
            pltpu.VMEM((RING, RING * lags, chans), F32),
            pltpu.VMEM((2, 4, RING * lags, chans), BF16),
            pltpu.VMEM((2, 4, RING * lags, chans), BF16),
            pltpu.VMEM((RING, lags, chans), F32),
            pltpu.VMEM((2, 4, lags, chans), F32),
            pltpu.VMEM((2, 4, lags, chans), F32),
            dma((12,)),
            dma((2,)),
            dma((2,)),
            dma((2, 2, 4)),
            dma((2, 2, 4)),
            dma((2, 2, 20)),
            dma((2, 2, 20)),
            dma((len(UNITS),)),
            dma((len(UNITS),)),
            dma((RING, len(PARTS))),
            dma((len(PARTS), 4, 2)),
            dma((len(GROUPS), RING)),
            dma((len(GROUPS), 4, 2)),
            dma((2, 4)),
            dma((2, 4)),
            dma((2, 4)),
            dma((2, 4)),
        ],
        compiler_params=pltpu.CompilerParams(
            collective_id=0, has_side_effects=True, vmem_limit_bytes=56 * 1024 * 1024
        ),
    )(*args, *tables)


def solution(mesh):
    placed = (
        P("tm", "chan"),
        P("tm", "chan"),
        P("tm", "chan"),
        P(None, "chan"),
        P("tm", "chan"),
        P("tm", "chan"),
    )

    def program(values, gates, cotangent, kernel_taps, value_weight, gate_weight):
        fwd, inv = dft_tables(kernel_taps.shape[0])
        tables = (*split_table(fwd), *split_table(inv))
        norm_scale = 1.0 / math.sqrt(values.shape[0])
        return jax.shard_map(
            lambda *args: body(norm_scale, args[6:], *args[:6]),
            mesh=mesh,
            in_specs=placed + (P(),) * 4,
            out_specs=(P("tm", "chan"), P("tm", "chan")),
            check_vma=False,
        )(values, gates, cotangent, kernel_taps, value_weight, gate_weight, *tables)

    return program
```

```python
import functools
import math

import jax
import jax.numpy as jnp
import ml_dtypes
import numpy as np
from jax import lax
from jax.experimental import pallas as pl
from jax.experimental.pallas import tpu as pltpu
from jax.sharding import PartitionSpec as P

MESH = pl.DeviceIdType.MESH
BF16 = jnp.bfloat16
F32 = jnp.float32
RING = 8
SLOT = {0: 0, -1: 1, 1: 2, -2: 3, 2: 4, -3: 5, 3: 6, 4: 7}
GROUPS = ((0, 1), (1, 3), (3, 5), (5, 7), (7, 8))
PARTS = ((0, 5), (5, 8))
UNITS = [(color, slots, blocks) for slots in GROUPS for blocks in PARTS for color in (0, 1)]


def arrivals():
    found = []
    for way in (0, 1):
        for color in (0, 1):
            found += [(1, color, way, distance, 0) for distance in range(1, 5)]
            for distance in range(1, 5):
                for group, (low, high) in enumerate(GROUPS):
                    if distance < 4 or max(low, 4 * way) < min(high, 4 * way + 4):
                        found.append((2, color, way, distance, group))
    return sorted(found, key=lambda event: (event[3] + event[4], event[0], event[3]))


EVENTS = arrivals()
CHORES = (8, 20, 32, 44, 52, 60, 64, 68)


def split_table(table):
    high = table.astype(ml_dtypes.bfloat16)
    low = (table - high.astype(np.float64)).astype(ml_dtypes.bfloat16)
    return jnp.asarray(high), jnp.asarray(low)


def dft_tables(half):
    length = 2 * half
    step = np.arange(length)
    freq = np.arange(half)
    angle = (freq[:, None] * step[None, :] % length) * (2.0 * np.pi / length)
    cosine, sine = np.cos(angle), -np.sin(angle)
    sine[0] = np.where(step % 2 == 0, 1.0, -1.0)
    forward = np.concatenate([cosine, sine], 0)
    weight = np.full((length,), 2.0 / length)
    weight[0] = weight[half] = 1.0 / length
    inverse = (forward[:, :half] * weight[:, None]).T
    return forward, inverse


def wrap(index):
    return lax.rem(index + RING, RING)


def slot_of(distance):
    far = lax.div(distance, 4)
    return (1 - far) * 2 * distance + far * (15 - 2 * distance)


def mm(left, right):
    return jnp.dot(left, right, preferred_element_type=F32)


def kernel(
    norm_scale,
    values_in,
    gates_in,
    cotangent_in,
    taps_in,
    value_weight,
    gate_weight,
    fwd_hi_in,
    fwd_lo_in,
    inv_hi_in,
    inv_lo_in,
    out,
    kernel_grad,
    values,
    gates,
    cotangent,
    taps,
    fwd_hi,
    fwd_lo,
    inv_hi,
    inv_lo,
    gather_a,
    gather_b,
    value_rim,
    grad_win,
    spec_v,
    spec_g,
    spec_p,
    spec_t,
    prod_hi,
    prod_lo,
    left_v,
    left_g,
    part_a,
    part_b,
    sib_a,
    sib_b,
    got_a,
    got_b,
    lag_part,
    kz_send,
    kz_got,
    lag_row,
    ky_send,
    ky_got,
    local_sem,
    rim_send_sem,
    rim_recv_sem,
    p1_send,
    p1_recv,
    p2_send,
    p2_recv,
    sib_send,
    sib_recv,
    a_send,
    a_recv,
    b_send,
    b_recv,
    kz_send_sem,
    kz_recv_sem,
    ky_send_sem,
    ky_recv_sem,
):
    rows = values.shape[0]
    tm = lax.axis_index("tm")
    me = lax.axis_index("chan")
    z, y = lax.div(tm, RING), lax.rem(tm, RING)

    def at_y(distance):
        return z * RING + wrap(y + distance)

    def at_z(distance):
        return wrap(z + distance) * RING + y

    def remote(src, dst, send_sem, recv_sem, axis, index):
        return pltpu.make_async_remote_copy(
            src_ref=src,
            dst_ref=dst,
            send_sem=send_sem,
            recv_sem=recv_sem,
            device_id={axis: index},
            device_id_type=MESH,
        )

    barrier = pltpu.get_barrier_semaphore()

    def greet(axis, index):
        pl.semaphore_signal(barrier, inc=1, device_id={axis: index}, device_id_type=MESH)

    half = value_weight.shape[0] // 2
    loads = []

    def load(src, dst):
        copy = pltpu.make_async_copy(src, dst, local_sem.at[len(loads)])
        copy.start()
        loads.append(copy)
        return copy

    own_rows = [
        load(weight.at[pl.ds(half * color, half)], gather.at[0, 0, which])
        for color, gather in ((0, gather_a), (1, gather_b))
        for which, weight in ((0, value_weight), (1, gate_weight))
    ]
    for distance in range(1, RING):
        greet("chan", wrap(me + distance))
    for distance in (-1, 1):
        greet("tm", at_y(distance))
        greet("tm", at_z(distance))
    after = lax.rem(tm + 1, RING * RING)
    before = lax.rem(tm + RING * RING - 1, RING * RING)
    greet("tm", after)
    greet("tm", before)
    streams = [load(cotangent_in, cotangent), load(gates_in, gates), load(values_in, values)]
    ahead = [load(taps_in, taps), load(fwd_hi_in, fwd_hi), load(fwd_lo_in, fwd_lo)]
    later = [load(inv_hi_in, inv_hi), load(inv_lo_in, inv_lo)]

    pl.semaphore_wait(barrier, (RING - 1) + 6)
    for copy in own_rows:
        copy.wait()

    sends = []

    def go(copy):
        copy.start()
        sends.append(copy)
        return copy

    buffers = (gather_a, gather_b)
    first_axis = (at_y, at_z)
    second_axis = (at_z, at_y)
    flights = {}

    def send1(color, way, distance):
        sign = -1 if way == 0 else 1
        src = buffers[color].at[0, SLOT[sign * distance]]
        if distance < 3:
            dst = buffers[color].at[0, SLOT[sign * (distance + 1)]]
        else:
            src, dst = src.at[way], buffers[color].at[0, SLOT[4], way]
        flights[1, color, way, distance + 1, 0] = go(
            remote(
                src,
                dst,
                p1_send.at[color, way, distance],
                p1_recv.at[color, way, distance],
                "tm",
                first_axis[color](-sign),
            )
        )

    def send2(color, way, distance, group):
        sign = -1 if way == 0 else 1
        low, high = GROUPS[group]
        target, at = SLOT[4], 15 + group
        if distance < 3:
            target, at = SLOT[sign * (distance + 1)], 5 * distance + group
        else:
            low, high = max(low, 4 * way), min(high, 4 * way + 4)
            if low >= high:
                return
        blocks = pl.ds(low, high - low)
        flights[2, color, way, distance + 1, group] = go(
            remote(
                buffers[color].at[SLOT[sign * distance], blocks],
                buffers[color].at[target, blocks],
                p2_send.at[color, way, at],
                p2_recv.at[color, way, at],
                "tm",
                second_axis[color](-sign),
            )
        )

    pairs = [(color, way) for way in (0, 1) for color in (0, 1)]

    def serve(event):
        stage, color, way, distance, group = event
        flights[event].wait_recv()
        if stage == 1:
            if distance < 4:
                send1(color, way, distance)
            if way == 1:
                for out_way in (0, 1):
                    send2(color, out_way, 0, distance)
        elif distance < 4:
            send2(color, way, distance, group)

    for color, way in pairs:
        send1(color, way, 0)
        send2(color, way, 0, 0)

    for copy in streams:
        copy.wait()
    grad_win[:rows] = (cotangent[...].astype(F32) * gates[...].astype(F32)).astype(BF16)
    rim_v = go(remote(values, value_rim, rim_send_sem.at[0], rim_recv_sem.at[0], "tm", after))
    rim_g = go(
        remote(
            grad_win.at[:rows], grad_win.at[rows:], rim_send_sem.at[1], rim_recv_sem.at[1], "tm", before
        )
    )

    def forward(first, data):
        cols = slice(0, rows) if first else slice(rows, 2 * rows)
        return mm(fwd_hi[:, cols], data) + mm(fwd_lo[:, cols], data)

    steps = {}
    for event in EVENTS:
        steps.setdefault(event[3] + event[4], []).append(event)

    for copy in ahead:
        copy.wait()
    spec_t[...] = forward(True, taps[...])
    spec_p[...] = forward(True, grad_win[:rows])
    for event in steps[1]:
        serve(event)
    spec_v[...] = forward(False, values[...])
    for event in steps[2]:
        serve(event)
    rim_v.wait_recv()
    has_before = (tm > 0).astype(F32)
    spec_v[...] = spec_v[...] + forward(True, value_rim[...]) * has_before
    rim_g.wait_recv()
    has_after = (tm < RING * RING - 1).astype(F32)
    spec_g[...] = spec_p[...] + forward(False, grad_win[rows:]) * has_after

    chans = values.shape[1]
    width = 128
    row_at = lax.broadcasted_iota(jnp.int32, (rows, width), 0)
    first_row = row_at == 0
    sign = (1 - 2 * (row_at & 1)).astype(F32)

    def product(left_re, left_im, right_re, right_im, flip):
        cross = left_im * right_im
        real = left_re * right_re
        if flip:
            imag = left_im * right_re - left_re * right_im
            real = real + jnp.where(first_row, 0.0, cross)
        else:
            imag = left_im * right_re + left_re * right_im
            real = real - jnp.where(first_row, 0.0, cross)
        return real, jnp.where(first_row, cross, imag)

    def keep(real, imag, at):
        for part, data in ((slice(0, rows), real), (slice(rows, 2 * rows), imag)):
            high = data.astype(BF16)
            prod_hi[part, at : at + width] = high
            prod_lo[part, at : at + width] = (data - high.astype(F32)).astype(BF16)

    for col in range(0, chans, width):
        cut = slice(col, col + width)
        v_re, v_im = spec_v[:rows, cut], spec_v[rows:, cut]
        t_re, t_im = spec_t[:rows, cut], spec_t[rows:, cut]
        g_re, g_im = spec_g[:rows, cut], spec_g[rows:, cut]
        p_re, p_im = spec_p[:rows, cut] * sign, spec_p[rows:, cut] * sign
        real, imag = product(v_re, v_im, t_re, t_im, False)
        keep(real * sign, imag * sign, col)
        real, imag = product(g_re, g_im, t_re, t_im, True)
        keep(real, imag, chans + col)
        real, imag = product(p_re, p_im, v_re, v_im, True)
        keep(real, imag, 2 * chans + col)

    def backward(index):
        cut = slice(index * chans, (index + 1) * chans)
        return (
            mm(inv_hi[...], prod_hi[:, cut])
            + mm(inv_hi[...], prod_lo[:, cut])
            + mm(inv_lo[...], prod_hi[:, cut])
        )

    def chain(own, send, got, send_sem, recv_sem, place, to):
        flying = {}

        def step(index):
            arrived = []
            for way, (length, sign) in enumerate(((3, 1), (4, -1))):
                if index > length:
                    continue
                if index:
                    flying[way, index - 1].wait_recv()
                    data = got[way, index - 1].astype(F32)
                if index == length:
                    flying[way] = data
                    continue
                mine = own[wrap(place + sign * (length - index))]
                if index:
                    mine = mine + data
                send[way, index] = mine.astype(send.dtype)
                flying[way, index] = go(
                    remote(
                        send.at[way, index],
                        got.at[way, index],
                        send_sem.at[way, index],
                        recv_sem.at[way, index],
                        "tm",
                        to(sign),
                    )
                )
            if index == 4:
                return own[place] + flying[0] + flying[1]

        return step

    for copy in later:
        copy.wait()
    lag_part[...] = (backward(2) * norm_scale).reshape(lag_part.shape)
    along_z = chain(lag_part, kz_send, kz_got, kz_send_sem, kz_recv_sem, z, at_z)
    along_y = chain(lag_row, ky_send, ky_got, ky_send_sem, ky_recv_sem, y, at_y)
    along_z(0)

    def chore(index):
        if index < 4:
            along_z(index)
        elif index == 4:
            total = along_z(4)
            lags = lag_row.shape[1]
            for at in range(RING):
                lag_row[at] = total[at * lags : (at + 1) * lags]
            along_y(0)
        elif index < 8:
            along_y(index - 4)
        else:
            kernel_grad[...] = along_y(4)

    left_v[...] = backward(1).T.astype(BF16)
    left_g[...] = (cotangent[...].astype(F32) * backward(0)).T.astype(BF16)

    parts = (part_a, part_b)
    pairs_got = (sib_a, sib_b)
    core = lax.rem(me, 2)
    chip = lax.div(me, 2)
    sibling = me + 1 - 2 * core

    def multiply(unit):
        color, slots, blocks = unit
        ref = buffers[color]
        shape = (slots[1] - slots[0], blocks[1] - blocks[0], 2, half // 2, rows)
        count = shape[0] * shape[1] * half
        cut = (slice(*slots), slice(*blocks))
        total = mm(ref[(*cut, 0)].reshape(count, chans), left_v[...])
        total = total + mm(ref[(*cut, 1)].reshape(count, chans), left_g[...])
        parts[color][cut] = total.astype(BF16).reshape(shape)
        at = (pl.ds(slots[0], shape[0]), pl.ds(blocks[0], shape[1]))
        index = UNITS.index(unit)
        return go(
            remote(
                parts[color].at[(*at, 1 - core)],
                pairs_got[color].at[at],
                sib_send.at[index],
                sib_recv.at[index],
                "chan",
                sibling,
            )
        )

    places = {slot: place for place, slot in SLOT.items()}

    def deliveries(unit):
        color, slots, blocks = unit
        group = GROUPS.index(slots)
        part = PARTS.index(blocks)
        found = []
        for slot in range(*(slots if color == 0 else blocks)):
            owner = wrap(z + places[slot])
            at = lax.rem(chip - lax.div(owner, 2) + 4, 4)
            if color == 0:
                lines = pl.ds(blocks[0], blocks[1] - blocks[0])
                src = part_a.at[slot, lines, core]
                dst = got_a.at[at, core, lines]
                sems = a_send.at[slot, part], a_recv.at[part, at, core]
            else:
                lines = pl.ds(slots[0], slots[1] - slots[0])
                src = part_b.at[lines, slot, core]
                dst = got_b.at[at, core, lines]
                sems = b_send.at[group, slot], b_recv.at[group, at, core]
            found.append((owner, src, dst, remote(src, dst, *sems, "chan", owner)))
        return found

    def finish(unit, flight):
        color, slots, blocks = unit
        flight.wait_recv()
        cut = (slice(*slots), slice(*blocks))
        total = parts[color][(*cut, core)].astype(F32) + pairs_got[color][cut].astype(F32)
        parts[color][(*cut, core)] = total.astype(BF16)
        for owner, src, dst, copy in deliveries(unit):

            @pl.when(owner != me)
            def _():
                copy.start()

            @pl.when(owner == me)
            def _():
                dst[...] = src[...]

    def needs(unit):
        color, slots, blocks = unit
        found = set()
        for slot in range(*slots):
            for block in range(*blocks):
                if slot == 0:
                    place = places[block]
                    ways = (0, 1) if place == 4 else (0,) if place < 0 else (1,)
                    if place:
                        found |= {(1, color, way, abs(place), 0) for way in ways}
                else:
                    way = (0 if block < 4 else 1) if slot == 7 else (0 if places[slot] < 0 else 1)
                    group = [low <= block < high for low, high in GROUPS].index(True)
                    found.add((2, color, way, abs(places[slot]), group))
        return found

    served = set(steps[1]) | set(steps[2])
    waiting = list(UNITS)
    pending = []

    def work():
        for unit in list(waiting):
            if needs(unit) <= served:
                waiting.remove(unit)
                pending.append((unit, multiply(unit)))
                if len(pending) > 1:
                    finish(*pending.pop(0))

    work()
    rest = [event for event in EVENTS if event not in served]
    for index, event in enumerate(rest):
        serve(event)
        served.add(event)
        work()
        if index + 1 in CHORES:
            chore(CHORES.index(index + 1) + 1)
    assert not waiting
    for unit, flight in pending:
        finish(unit, flight)

    for at in range(4):
        for which in (0, 1) if at else (1 - core,):
            for part, (low, high) in enumerate(PARTS):
                lines = pl.ds(low, high - low)
                remote(
                    part_a.at[0, lines, 0],
                    got_a.at[at, which, lines],
                    a_send.at[0, part],
                    a_recv.at[part, at, which],
                    "chan",
                    sibling,
                ).wait_recv()
            for group, (low, high) in enumerate(GROUPS):
                lines = pl.ds(low, high - low)
                remote(
                    part_b.at[lines, 0, 0],
                    got_b.at[at, which, lines],
                    b_send.at[group, 0],
                    b_recv.at[group, at, which],
                    "chan",
                    sibling,
                ).wait_recv()

    for pair in range(RING // 2):
        pieces = []
        for place in (2 * pair, 2 * pair + 1):
            block = slot_of(wrap(place - y))
            for got in (got_a, got_b):
                for which in (0, 1):
                    total = got[0, which, block].astype(F32)
                    for at in range(1, 4):
                        total = total + got[at, which, block].astype(F32)
                    pieces.append(total)
        merged = jnp.concatenate(pieces, 0)
        out[:, 4 * half * pair : 4 * half * (pair + 1)] = merged.T.astype(BF16)

    for copy in sends:
        copy.wait_send()
    for unit in UNITS:
        for owner, src, dst, copy in deliveries(unit):

            @pl.when(owner != me)
            def _():
                copy.wait_send()


def body(norm_scale, tables, *args):
    values, _, _, taps, value_weight, _ = args
    rows, chans = values.shape
    half = value_weight.shape[0] // 2
    lags = taps.shape[0] // (RING * RING)
    assert taps.shape[0] == rows and lax.axis_size("tm") == RING * RING
    assert lax.axis_size("chan") == RING and chans == RING * 2 * half
    vmem = pl.BlockSpec(memory_space=pltpu.VMEM)
    dma = pltpu.SemaphoreType.DMA
    done = pl.pallas_call(
        functools.partial(kernel, norm_scale),
        out_shape=(
            jax.ShapeDtypeStruct((rows, chans), BF16),
            jax.ShapeDtypeStruct((lags, chans), F32),
        ),
        in_specs=[pl.BlockSpec(memory_space=pl.ANY)] * 10,
        out_specs=(vmem, vmem),
        scratch_shapes=[
            pltpu.VMEM((rows, chans), BF16),
            pltpu.VMEM((rows, chans), BF16),
            pltpu.VMEM((rows, chans), BF16),
            pltpu.VMEM((rows, chans), BF16),
            *(pltpu.VMEM(table.shape, BF16) for table in tables),
            pltpu.VMEM((RING, RING, 2, half, chans), BF16),
            pltpu.VMEM((RING, RING, 2, half, chans), BF16),
            pltpu.VMEM((rows, chans), BF16),
            pltpu.VMEM((2 * rows, chans), BF16),
            pltpu.VMEM((2 * rows, chans), F32),
            pltpu.VMEM((2 * rows, chans), F32),
            pltpu.VMEM((2 * rows, chans), F32),
            pltpu.VMEM((2 * rows, chans), F32),
            pltpu.VMEM((2 * rows, 3 * chans), BF16),
            pltpu.VMEM((2 * rows, 3 * chans), BF16),
            pltpu.VMEM((chans, rows), BF16),
            pltpu.VMEM((chans, rows), BF16),
            pltpu.VMEM((RING, RING, 2, half // 2, rows), BF16),
            pltpu.VMEM((RING, RING, 2, half // 2, rows), BF16),
            pltpu.VMEM((RING, RING, half // 2, rows), BF16),
            pltpu.VMEM((RING, RING, half // 2, rows), BF16),
            pltpu.VMEM((4, 2, RING, half // 2, rows), BF16),
            pltpu.VMEM((4, 2, RING, half // 2, rows), BF16),
            pltpu.VMEM((RING, RING * lags, chans), F32),
            pltpu.VMEM((2, 4, RING * lags, chans), BF16),
            pltpu.VMEM((2, 4, RING * lags, chans), BF16),
            pltpu.VMEM((RING, lags, chans), F32),
            pltpu.VMEM((2, 4, lags, chans), F32),
            pltpu.VMEM((2, 4, lags, chans), F32),
            dma((12,)),
            dma((2,)),
            dma((2,)),
            dma((2, 2, 4)),
            dma((2, 2, 4)),
            dma((2, 2, 20)),
            dma((2, 2, 20)),
            dma((len(UNITS),)),
            dma((len(UNITS),)),
            dma((RING, len(PARTS))),
            dma((len(PARTS), 4, 2)),
            dma((len(GROUPS), RING)),
            dma((len(GROUPS), 4, 2)),
            dma((2, 4)),
            dma((2, 4)),
            dma((2, 4)),
            dma((2, 4)),
        ],
        compiler_params=pltpu.CompilerParams(
            collective_id=0, has_side_effects=True, vmem_limit_bytes=56 * 1024 * 1024
        ),
    )(*args, *tables)

    cuts = 4

    def hand_out(total, lags_in, out, lags_out, sem):
        copies = [pltpu.make_async_copy(lags_in, lags_out, sem.at[cuts])]
        for index in range(cuts):
            part = pl.ds(index * (rows // cuts), rows // cuts)
            copies.append(pltpu.make_async_copy(total.at[part], out.at[part], sem.at[index]))
        for copy in copies:
            copy.start()
        for copy in copies:
            copy.wait()

    anywhere = pl.BlockSpec(memory_space=pl.ANY)
    return pl.pallas_call(
        hand_out,
        out_shape=tuple(jax.ShapeDtypeStruct(array.shape, array.dtype) for array in done),
        in_specs=[anywhere, anywhere],
        out_specs=(anywhere, anywhere),
        scratch_shapes=[dma((cuts + 1,))],
    )(*done)


def solution(mesh):
    placed = (
        P("tm", "chan"),
        P("tm", "chan"),
        P("tm", "chan"),
        P(None, "chan"),
        P("tm", "chan"),
        P("tm", "chan"),
    )

    def program(values, gates, cotangent, kernel_taps, value_weight, gate_weight):
        fwd, inv = dft_tables(kernel_taps.shape[0])
        tables = (*split_table(fwd), *split_table(inv))
        norm_scale = 1.0 / math.sqrt(values.shape[0])
        return jax.shard_map(
            lambda *args: body(norm_scale, args[6:], *args[:6]),
            mesh=mesh,
            in_specs=placed + (P(),) * 4,
            out_specs=(P("tm", "chan"), P("tm", "chan")),
            check_vma=False,
        )(values, gates, cotangent, kernel_taps, value_weight, gate_weight, *tables)

    return program
```

```python
import functools
import math

import jax
import jax.numpy as jnp
import ml_dtypes
import numpy as np
from jax import lax
from jax.experimental import pallas as pl
from jax.experimental.pallas import tpu as pltpu
from jax.sharding import PartitionSpec as P

MESH = pl.DeviceIdType.MESH
BF16 = jnp.bfloat16
F32 = jnp.float32
RING = 8
SLOT = {0: 0, -1: 1, 1: 2, -2: 3, 2: 4, -3: 5, 3: 6, 4: 7}
GROUPS = ((0, 1), (1, 3), (3, 5), (5, 7), (7, 8))
PARTS = ((0, 5), (5, 8))
UNITS = [(color, slots, blocks) for slots in GROUPS for blocks in PARTS for color in (0, 1)]


def arrivals():
    found = []
    for way in (0, 1):
        for color in (0, 1):
            found += [(1, color, way, distance, 0) for distance in range(1, 5)]
            for distance in range(1, 5):
                for group, (low, high) in enumerate(GROUPS):
                    if distance < 4 or max(low, 4 * way) < min(high, 4 * way + 4):
                        found.append((2, color, way, distance, group))
    return sorted(found, key=lambda event: (event[3] + event[4], event[0], event[3]))


EVENTS = arrivals()
CHORES = (8, 20, 32, 44, 52, 60, 64, 68)


def split_table(table):
    high = table.astype(ml_dtypes.bfloat16)
    low = (table - high.astype(np.float64)).astype(ml_dtypes.bfloat16)
    return jnp.asarray(high), jnp.asarray(low)


def dft_tables(half):
    length = 2 * half
    step = np.arange(length)
    freq = np.arange(half)
    angle = (freq[:, None] * step[None, :] % length) * (2.0 * np.pi / length)
    cosine, sine = np.cos(angle), -np.sin(angle)
    sine[0] = np.where(step % 2 == 0, 1.0, -1.0)
    forward = np.concatenate([cosine, sine], 0)
    weight = np.full((length,), 2.0 / length)
    weight[0] = weight[half] = 1.0 / length
    inverse = (forward[:, :half] * weight[:, None]).T
    return forward, inverse


def wrap(index):
    return lax.rem(index + RING, RING)


def slot_of(distance):
    far = lax.div(distance, 4)
    return (1 - far) * 2 * distance + far * (15 - 2 * distance)


def mm(left, right):
    return jnp.dot(left, right, preferred_element_type=F32)


def kernel(
    norm_scale,
    values_in,
    gates_in,
    cotangent_in,
    taps_in,
    value_weight,
    gate_weight,
    fwd_hi_in,
    fwd_lo_in,
    inv_hi_in,
    inv_lo_in,
    out,
    kernel_grad,
    values,
    gates,
    cotangent,
    taps,
    fwd_hi,
    fwd_lo,
    inv_hi,
    inv_lo,
    gather_a,
    gather_b,
    value_rim,
    grad_win,
    spec_v,
    spec_g,
    spec_p,
    spec_t,
    prod_hi,
    prod_lo,
    left_v,
    left_g,
    part_a,
    part_b,
    sib_a,
    sib_b,
    got_a,
    got_b,
    lag_part,
    kz_send,
    kz_got,
    lag_row,
    ky_send,
    ky_got,
    local_sem,
    rim_send_sem,
    rim_recv_sem,
    p1_send,
    p1_recv,
    p2_send,
    p2_recv,
    sib_send,
    sib_recv,
    a_send,
    a_recv,
    b_send,
    b_recv,
    kz_send_sem,
    kz_recv_sem,
    ky_send_sem,
    ky_recv_sem,
):
    rows = values.shape[0]
    tm = lax.axis_index("tm")
    me = lax.axis_index("chan")
    z, y = lax.div(tm, RING), lax.rem(tm, RING)

    def at_y(distance):
        return z * RING + wrap(y + distance)

    def at_z(distance):
        return wrap(z + distance) * RING + y

    def remote(src, dst, send_sem, recv_sem, axis, index):
        return pltpu.make_async_remote_copy(
            src_ref=src,
            dst_ref=dst,
            send_sem=send_sem,
            recv_sem=recv_sem,
            device_id={axis: index},
            device_id_type=MESH,
        )

    barrier = pltpu.get_barrier_semaphore()

    def greet(axis, index):
        pl.semaphore_signal(barrier, inc=1, device_id={axis: index}, device_id_type=MESH)

    half = value_weight.shape[0] // 2
    loads = []

    def load(src, dst):
        copy = pltpu.make_async_copy(src, dst, local_sem.at[len(loads)])
        copy.start()
        loads.append(copy)
        return copy

    own_rows = [
        load(weight.at[pl.ds(half * color, half)], gather.at[0, 0, which])
        for color, gather in ((0, gather_a), (1, gather_b))
        for which, weight in ((0, value_weight), (1, gate_weight))
    ]
    for distance in range(1, RING):
        greet("chan", wrap(me + distance))
    for distance in (-1, 1):
        greet("tm", at_y(distance))
        greet("tm", at_z(distance))
    after = lax.rem(tm + 1, RING * RING)
    before = lax.rem(tm + RING * RING - 1, RING * RING)
    greet("tm", after)
    greet("tm", before)
    streams = [load(cotangent_in, cotangent), load(gates_in, gates), load(values_in, values)]
    ahead = [load(taps_in, taps), load(fwd_hi_in, fwd_hi), load(fwd_lo_in, fwd_lo)]
    later = [load(inv_hi_in, inv_hi), load(inv_lo_in, inv_lo)]

    pl.semaphore_wait(barrier, (RING - 1) + 6)
    for copy in own_rows:
        copy.wait()

    sends = []

    def go(copy):
        copy.start()
        sends.append(copy)
        return copy

    buffers = (gather_a, gather_b)
    first_axis = (at_y, at_z)
    second_axis = (at_z, at_y)
    flights = {}

    def send1(color, way, distance):
        sign = -1 if way == 0 else 1
        src = buffers[color].at[0, SLOT[sign * distance]]
        if distance < 3:
            dst = buffers[color].at[0, SLOT[sign * (distance + 1)]]
        else:
            src, dst = src.at[way], buffers[color].at[0, SLOT[4], way]
        flights[1, color, way, distance + 1, 0] = go(
            remote(
                src,
                dst,
                p1_send.at[color, way, distance],
                p1_recv.at[color, way, distance],
                "tm",
                first_axis[color](-sign),
            )
        )

    def send2(color, way, distance, group):
        sign = -1 if way == 0 else 1
        low, high = GROUPS[group]
        target, at = SLOT[4], 15 + group
        if distance < 3:
            target, at = SLOT[sign * (distance + 1)], 5 * distance + group
        else:
            low, high = max(low, 4 * way), min(high, 4 * way + 4)
            if low >= high:
                return
        blocks = pl.ds(low, high - low)
        flights[2, color, way, distance + 1, group] = go(
            remote(
                buffers[color].at[SLOT[sign * distance], blocks],
                buffers[color].at[target, blocks],
                p2_send.at[color, way, at],
                p2_recv.at[color, way, at],
                "tm",
                second_axis[color](-sign),
            )
        )

    pairs = [(color, way) for way in (0, 1) for color in (0, 1)]

    def serve(event):
        stage, color, way, distance, group = event
        flights[event].wait_recv()
        if stage == 1:
            if distance < 4:
                send1(color, way, distance)
            if way == 1:
                for out_way in (0, 1):
                    send2(color, out_way, 0, distance)
        elif distance < 4:
            send2(color, way, distance, group)

    for color, way in pairs:
        send1(color, way, 0)
        send2(color, way, 0, 0)

    for copy in streams:
        copy.wait()
    grad_win[:rows] = (cotangent[...].astype(F32) * gates[...].astype(F32)).astype(BF16)
    rim_v = go(remote(values, value_rim, rim_send_sem.at[0], rim_recv_sem.at[0], "tm", after))
    rim_g = go(
        remote(
            grad_win.at[:rows], grad_win.at[rows:], rim_send_sem.at[1], rim_recv_sem.at[1], "tm", before
        )
    )

    def forward(first, data):
        cols = slice(0, rows) if first else slice(rows, 2 * rows)
        return mm(fwd_hi[:, cols], data) + mm(fwd_lo[:, cols], data)

    steps = {}
    for event in EVENTS:
        steps.setdefault(event[3] + event[4], []).append(event)

    for copy in ahead:
        copy.wait()
    spec_t[...] = forward(True, taps[...])
    spec_p[...] = forward(True, grad_win[:rows])
    for event in steps[1]:
        serve(event)
    spec_v[...] = forward(False, values[...])
    for event in steps[2]:
        serve(event)
    rim_v.wait_recv()
    has_before = (tm > 0).astype(F32)
    spec_v[...] = spec_v[...] + forward(True, value_rim[...]) * has_before
    rim_g.wait_recv()
    has_after = (tm < RING * RING - 1).astype(F32)
    spec_g[...] = spec_p[...] + forward(False, grad_win[rows:]) * has_after

    chans = values.shape[1]
    width = 128
    row_at = lax.broadcasted_iota(jnp.int32, (rows, width), 0)
    first_row = row_at == 0
    sign = (1 - 2 * (row_at & 1)).astype(F32)

    def product(left_re, left_im, right_re, right_im, flip):
        cross = left_im * right_im
        real = left_re * right_re
        if flip:
            imag = left_im * right_re - left_re * right_im
            real = real + jnp.where(first_row, 0.0, cross)
        else:
            imag = left_im * right_re + left_re * right_im
            real = real - jnp.where(first_row, 0.0, cross)
        return real, jnp.where(first_row, cross, imag)

    def keep(real, imag, at):
        for part, data in ((slice(0, rows), real), (slice(rows, 2 * rows), imag)):
            high = data.astype(BF16)
            prod_hi[part, at : at + width] = high
            prod_lo[part, at : at + width] = (data - high.astype(F32)).astype(BF16)

    for col in range(0, chans, width):
        cut = slice(col, col + width)
        v_re, v_im = spec_v[:rows, cut], spec_v[rows:, cut]
        t_re, t_im = spec_t[:rows, cut], spec_t[rows:, cut]
        g_re, g_im = spec_g[:rows, cut], spec_g[rows:, cut]
        p_re, p_im = spec_p[:rows, cut] * sign, spec_p[rows:, cut] * sign
        real, imag = product(v_re, v_im, t_re, t_im, False)
        keep(real * sign, imag * sign, col)
        real, imag = product(g_re, g_im, t_re, t_im, True)
        keep(real, imag, chans + col)
        real, imag = product(p_re, p_im, v_re, v_im, True)
        keep(real, imag, 2 * chans + col)

    def backward(index):
        cut = slice(index * chans, (index + 1) * chans)
        return (
            mm(inv_hi[...], prod_hi[:, cut])
            + mm(inv_hi[...], prod_lo[:, cut])
            + mm(inv_lo[...], prod_hi[:, cut])
        )

    def chain(own, send, got, send_sem, recv_sem, place, to):
        flying = {}

        def step(index):
            arrived = []
            for way, (length, sign) in enumerate(((3, 1), (4, -1))):
                if index > length:
                    continue
                if index:
                    flying[way, index - 1].wait_recv()
                    data = got[way, index - 1].astype(F32)
                if index == length:
                    flying[way] = data
                    continue
                mine = own[wrap(place + sign * (length - index))]
                if index:
                    mine = mine + data
                send[way, index] = mine.astype(send.dtype)
                flying[way, index] = go(
                    remote(
                        send.at[way, index],
                        got.at[way, index],
                        send_sem.at[way, index],
                        recv_sem.at[way, index],
                        "tm",
                        to(sign),
                    )
                )
            if index == 4:
                return own[place] + flying[0] + flying[1]

        return step

    for copy in later:
        copy.wait()
    lag_part[...] = (backward(2) * norm_scale).reshape(lag_part.shape)
    along_z = chain(lag_part, kz_send, kz_got, kz_send_sem, kz_recv_sem, z, at_z)
    along_y = chain(lag_row, ky_send, ky_got, ky_send_sem, ky_recv_sem, y, at_y)
    along_z(0)

    def chore(index):
        if index < 4:
            along_z(index)
        elif index == 4:
            total = along_z(4)
            lags = lag_row.shape[1]
            for at in range(RING):
                lag_row[at] = total[at * lags : (at + 1) * lags]
            along_y(0)
        elif index < 8:
            along_y(index - 4)
        else:
            kernel_grad[...] = along_y(4)

    left_v[...] = backward(1).T.astype(BF16)
    left_g[...] = (cotangent[...].astype(F32) * backward(0)).T.astype(BF16)

    parts = (part_a, part_b)
    pairs_got = (sib_a, sib_b)
    core = lax.rem(me, 2)
    chip = lax.div(me, 2)
    sibling = me + 1 - 2 * core

    def multiply(unit):
        color, slots, blocks = unit
        ref = buffers[color]
        shape = (slots[1] - slots[0], blocks[1] - blocks[0], 2, half // 2, rows)
        count = shape[0] * shape[1] * half
        cut = (slice(*slots), slice(*blocks))
        total = mm(ref[(*cut, 0)].reshape(count, chans), left_v[...])
        total = total + mm(ref[(*cut, 1)].reshape(count, chans), left_g[...])
        parts[color][cut] = total.astype(BF16).reshape(shape)
        at = (pl.ds(slots[0], shape[0]), pl.ds(blocks[0], shape[1]))
        index = UNITS.index(unit)
        return go(
            remote(
                parts[color].at[(*at, 1 - core)],
                pairs_got[color].at[at],
                sib_send.at[index],
                sib_recv.at[index],
                "chan",
                sibling,
            )
        )

    places = {slot: place for place, slot in SLOT.items()}

    def deliveries(unit):
        color, slots, blocks = unit
        group = GROUPS.index(slots)
        part = PARTS.index(blocks)
        found = []
        for slot in range(*(slots if color == 0 else blocks)):
            owner = wrap(z + places[slot])
            at = lax.rem(chip - lax.div(owner, 2) + 4, 4)
            if color == 0:
                lines = pl.ds(blocks[0], blocks[1] - blocks[0])
                src = part_a.at[slot, lines, core]
                dst = got_a.at[at, core, lines]
                sems = a_send.at[slot, part], a_recv.at[part, at, core]
            else:
                lines = pl.ds(slots[0], slots[1] - slots[0])
                src = part_b.at[lines, slot, core]
                dst = got_b.at[at, core, lines]
                sems = b_send.at[group, slot], b_recv.at[group, at, core]
            found.append((owner, src, dst, remote(src, dst, *sems, "chan", owner)))
        return found

    def finish(unit, flight):
        color, slots, blocks = unit
        flight.wait_recv()
        cut = (slice(*slots), slice(*blocks))
        total = parts[color][(*cut, core)].astype(F32) + pairs_got[color][cut].astype(F32)
        parts[color][(*cut, core)] = total.astype(BF16)
        for owner, src, dst, copy in deliveries(unit):

            @pl.when(owner != me)
            def _():
                copy.start()

            @pl.when(owner == me)
            def _():
                dst[...] = src[...]

    def needs(unit):
        color, slots, blocks = unit
        found = set()
        for slot in range(*slots):
            for block in range(*blocks):
                if slot == 0:
                    place = places[block]
                    ways = (0, 1) if place == 4 else (0,) if place < 0 else (1,)
                    if place:
                        found |= {(1, color, way, abs(place), 0) for way in ways}
                else:
                    way = (0 if block < 4 else 1) if slot == 7 else (0 if places[slot] < 0 else 1)
                    group = [low <= block < high for low, high in GROUPS].index(True)
                    found.add((2, color, way, abs(places[slot]), group))
        return found

    served = set(steps[1]) | set(steps[2])
    waiting = list(UNITS)
    pending = []

    def work():
        for unit in list(waiting):
            if needs(unit) <= served:
                waiting.remove(unit)
                pending.append((unit, multiply(unit)))
                if len(pending) > 1:
                    finish(*pending.pop(0))

    work()
    rest = [event for event in EVENTS if event not in served]
    for index, event in enumerate(rest):
        serve(event)
        served.add(event)
        work()
        if index + 1 in CHORES:
            chore(CHORES.index(index + 1) + 1)
    assert not waiting
    for unit, flight in pending:
        finish(unit, flight)

    for at in range(4):
        for which in (0, 1) if at else (1 - core,):
            for part, (low, high) in enumerate(PARTS):
                lines = pl.ds(low, high - low)
                remote(
                    part_a.at[0, lines, 0],
                    got_a.at[at, which, lines],
                    a_send.at[0, part],
                    a_recv.at[part, at, which],
                    "chan",
                    sibling,
                ).wait_recv()
            for group, (low, high) in enumerate(GROUPS):
                lines = pl.ds(low, high - low)
                remote(
                    part_b.at[lines, 0, 0],
                    got_b.at[at, which, lines],
                    b_send.at[group, 0],
                    b_recv.at[group, at, which],
                    "chan",
                    sibling,
                ).wait_recv()

    for pair in range(RING // 2):
        pieces = []
        for place in (2 * pair, 2 * pair + 1):
            block = slot_of(wrap(place - y))
            for got in (got_a, got_b):
                for which in (0, 1):
                    total = got[0, which, block].astype(F32)
                    for at in range(1, 4):
                        total = total + got[at, which, block].astype(F32)
                    pieces.append(total)
        merged = jnp.concatenate(pieces, 0)
        out[:, 4 * half * pair : 4 * half * (pair + 1)] = merged.T.astype(BF16)

    for copy in sends:
        copy.wait_send()
    for unit in UNITS:
        for owner, src, dst, copy in deliveries(unit):

            @pl.when(owner != me)
            def _():
                copy.wait_send()


def body(norm_scale, tables, *args):
    values, _, _, taps, value_weight, _ = args
    rows, chans = values.shape
    half = value_weight.shape[0] // 2
    lags = taps.shape[0] // (RING * RING)
    assert taps.shape[0] == rows and lax.axis_size("tm") == RING * RING
    assert lax.axis_size("chan") == RING and chans == RING * 2 * half
    vmem = pl.BlockSpec(memory_space=pltpu.VMEM)
    dma = pltpu.SemaphoreType.DMA
    done = pl.pallas_call(
        functools.partial(kernel, norm_scale),
        out_shape=(
            jax.ShapeDtypeStruct((rows, chans), BF16),
            jax.ShapeDtypeStruct((lags, chans), F32),
        ),
        in_specs=[pl.BlockSpec(memory_space=pl.ANY)] * 10,
        out_specs=(vmem, vmem),
        scratch_shapes=[
            pltpu.VMEM((rows, chans), BF16),
            pltpu.VMEM((rows, chans), BF16),
            pltpu.VMEM((rows, chans), BF16),
            pltpu.VMEM((rows, chans), BF16),
            *(pltpu.VMEM(table.shape, BF16) for table in tables),
            pltpu.VMEM((RING, RING, 2, half, chans), BF16),
            pltpu.VMEM((RING, RING, 2, half, chans), BF16),
            pltpu.VMEM((rows, chans), BF16),
            pltpu.VMEM((2 * rows, chans), BF16),
            pltpu.VMEM((2 * rows, chans), F32),
            pltpu.VMEM((2 * rows, chans), F32),
            pltpu.VMEM((2 * rows, chans), F32),
            pltpu.VMEM((2 * rows, chans), F32),
            pltpu.VMEM((2 * rows, 3 * chans), BF16),
            pltpu.VMEM((2 * rows, 3 * chans), BF16),
            pltpu.VMEM((chans, rows), BF16),
            pltpu.VMEM((chans, rows), BF16),
            pltpu.VMEM((RING, RING, 2, half // 2, rows), BF16),
            pltpu.VMEM((RING, RING, 2, half // 2, rows), BF16),
            pltpu.VMEM((RING, RING, half // 2, rows), BF16),
            pltpu.VMEM((RING, RING, half // 2, rows), BF16),
            pltpu.VMEM((4, 2, RING, half // 2, rows), BF16),
            pltpu.VMEM((4, 2, RING, half // 2, rows), BF16),
            pltpu.VMEM((RING, RING * lags, chans), F32),
            pltpu.VMEM((2, 4, RING * lags, chans), BF16),
            pltpu.VMEM((2, 4, RING * lags, chans), BF16),
            pltpu.VMEM((RING, lags, chans), F32),
            pltpu.VMEM((2, 4, lags, chans), F32),
            pltpu.VMEM((2, 4, lags, chans), F32),
            dma((12,)),
            dma((2,)),
            dma((2,)),
            dma((2, 2, 4)),
            dma((2, 2, 4)),
            dma((2, 2, 20)),
            dma((2, 2, 20)),
            dma((len(UNITS),)),
            dma((len(UNITS),)),
            dma((RING, len(PARTS))),
            dma((len(PARTS), 4, 2)),
            dma((len(GROUPS), RING)),
            dma((len(GROUPS), 4, 2)),
            dma((2, 4)),
            dma((2, 4)),
            dma((2, 4)),
            dma((2, 4)),
        ],
        compiler_params=pltpu.CompilerParams(
            collective_id=0, has_side_effects=True, vmem_limit_bytes=56 * 1024 * 1024
        ),
    )(*args, *tables)

    def hand_out(total, lags_in, out, lags_out):
        out[...] = total[...]
        lags_out[...] = lags_in[...]

    return pl.pallas_call(
        hand_out,
        out_shape=tuple(jax.ShapeDtypeStruct(array.shape, array.dtype) for array in done),
        in_specs=[vmem, vmem],
        out_specs=(vmem, vmem),
    )(*done)


def solution(mesh):
    placed = (
        P("tm", "chan"),
        P("tm", "chan"),
        P("tm", "chan"),
        P(None, "chan"),
        P("tm", "chan"),
        P("tm", "chan"),
    )

    def program(values, gates, cotangent, kernel_taps, value_weight, gate_weight):
        fwd, inv = dft_tables(kernel_taps.shape[0])
        tables = (*split_table(fwd), *split_table(inv))
        norm_scale = 1.0 / math.sqrt(values.shape[0])
        return jax.shard_map(
            lambda *args: body(norm_scale, args[6:], *args[:6]),
            mesh=mesh,
            in_specs=placed + (P(),) * 4,
            out_specs=(P("tm", "chan"), P("tm", "chan")),
            check_vma=False,
        )(values, gates, cotangent, kernel_taps, value_weight, gate_weight, *tables)

    return program
```

```python
import functools
import math

import jax
import jax.numpy as jnp
import ml_dtypes
import numpy as np
from jax import lax
from jax.experimental import pallas as pl
from jax.experimental.pallas import tpu as pltpu
from jax.sharding import PartitionSpec as P

MESH = pl.DeviceIdType.MESH
BF16 = jnp.bfloat16
F32 = jnp.float32
RING = 8
SLOT = {0: 0, -1: 1, 1: 2, -2: 3, 2: 4, -3: 5, 3: 6, 4: 7}
GROUPS = ((0, 1), (1, 3), (3, 5), (5, 7), (7, 8))
PARTS = ((0, 5), (5, 8))
UNITS = [(color, slots, blocks) for slots in GROUPS for blocks in PARTS for color in (0, 1)]


def arrivals():
    found = []
    for way in (0, 1):
        for color in (0, 1):
            found += [(1, color, way, distance, 0) for distance in range(1, 5)]
            for distance in range(1, 5):
                for group, (low, high) in enumerate(GROUPS):
                    if distance < 4 or max(low, 4 * way) < min(high, 4 * way + 4):
                        found.append((2, color, way, distance, group))
    return sorted(found, key=lambda event: (event[3] + event[4], event[0], event[3]))


EVENTS = arrivals()
CHORES = (8, 20, 32, 44, 52, 60, 64, 68)


def split_table(table):
    high = table.astype(ml_dtypes.bfloat16)
    low = (table - high.astype(np.float64)).astype(ml_dtypes.bfloat16)
    return jnp.asarray(high), jnp.asarray(low)


def dft_tables(half):
    length = 2 * half
    step = np.arange(length)
    freq = np.arange(half)
    angle = (freq[:, None] * step[None, :] % length) * (2.0 * np.pi / length)
    cosine, sine = np.cos(angle), -np.sin(angle)
    sine[0] = np.where(step % 2 == 0, 1.0, -1.0)
    forward = np.concatenate([cosine, sine], 0)
    weight = np.full((length,), 2.0 / length)
    weight[0] = weight[half] = 1.0 / length
    inverse = (forward[:, :half] * weight[:, None]).T
    return forward, inverse


def wrap(index):
    return lax.rem(index + RING, RING)


def slot_of(distance):
    far = lax.div(distance, 4)
    return (1 - far) * 2 * distance + far * (15 - 2 * distance)


def mm(left, right):
    return jnp.dot(left, right, preferred_element_type=F32)


def kernel(
    norm_scale,
    values_in,
    gates_in,
    cotangent_in,
    taps_in,
    value_weight,
    gate_weight,
    fwd_hi_in,
    fwd_lo_in,
    inv_hi_in,
    inv_lo_in,
    out,
    kernel_grad,
    values,
    gates,
    cotangent,
    taps,
    fwd_hi,
    fwd_lo,
    inv_hi,
    inv_lo,
    gather_a,
    gather_b,
    value_rim,
    grad_win,
    spec_v,
    spec_g,
    spec_p,
    spec_t,
    prod_hi,
    prod_lo,
    left_v,
    left_g,
    part_a,
    part_b,
    sib_a,
    sib_b,
    got_a,
    got_b,
    lag_part,
    kz_send,
    kz_got,
    lag_row,
    ky_send,
    ky_got,
    local_sem,
    rim_send_sem,
    rim_recv_sem,
    p1_send,
    p1_recv,
    p2_send,
    p2_recv,
    sib_send,
    sib_recv,
    a_send,
    a_recv,
    b_send,
    b_recv,
    kz_send_sem,
    kz_recv_sem,
    ky_send_sem,
    ky_recv_sem,
):
    rows = values.shape[0]
    tm = lax.axis_index("tm")
    me = lax.axis_index("chan")
    z, y = lax.div(tm, RING), lax.rem(tm, RING)

    def at_y(distance):
        return z * RING + wrap(y + distance)

    def at_z(distance):
        return wrap(z + distance) * RING + y

    def remote(src, dst, send_sem, recv_sem, axis, index):
        return pltpu.make_async_remote_copy(
            src_ref=src,
            dst_ref=dst,
            send_sem=send_sem,
            recv_sem=recv_sem,
            device_id={axis: index},
            device_id_type=MESH,
        )

    barrier = pltpu.get_barrier_semaphore()

    def greet(axis, index):
        pl.semaphore_signal(barrier, inc=1, device_id={axis: index}, device_id_type=MESH)

    half = value_weight.shape[0] // 2
    loads = []

    def load(src, dst):
        copy = pltpu.make_async_copy(src, dst, local_sem.at[len(loads)])
        copy.start()
        loads.append(copy)
        return copy

    own_rows = [
        load(weight.at[pl.ds(half * color, half)], gather.at[0, 0, which])
        for color, gather in ((0, gather_a), (1, gather_b))
        for which, weight in ((0, value_weight), (1, gate_weight))
    ]
    for distance in range(1, RING):
        greet("chan", wrap(me + distance))
    for distance in (-1, 1):
        greet("tm", at_y(distance))
        greet("tm", at_z(distance))
    after = lax.rem(tm + 1, RING * RING)
    before = lax.rem(tm + RING * RING - 1, RING * RING)
    greet("tm", after)
    greet("tm", before)
    streams = [load(cotangent_in, cotangent), load(gates_in, gates), load(values_in, values)]
    ahead = [load(taps_in, taps), load(fwd_hi_in, fwd_hi), load(fwd_lo_in, fwd_lo)]
    later = [load(inv_hi_in, inv_hi), load(inv_lo_in, inv_lo)]

    pl.semaphore_wait(barrier, (RING - 1) + 6)
    for copy in own_rows:
        copy.wait()

    sends = []

    def go(copy):
        copy.start()
        sends.append(copy)
        return copy

    buffers = (gather_a, gather_b)
    first_axis = (at_y, at_z)
    second_axis = (at_z, at_y)
    flights = {}

    def send1(color, way, distance):
        sign = -1 if way == 0 else 1
        src = buffers[color].at[0, SLOT[sign * distance]]
        if distance < 3:
            dst = buffers[color].at[0, SLOT[sign * (distance + 1)]]
        else:
            src, dst = src.at[way], buffers[color].at[0, SLOT[4], way]
        flights[1, color, way, distance + 1, 0] = go(
            remote(
                src,
                dst,
                p1_send.at[color, way, distance],
                p1_recv.at[color, way, distance],
                "tm",
                first_axis[color](-sign),
            )
        )

    def send2(color, way, distance, group):
        sign = -1 if way == 0 else 1
        low, high = GROUPS[group]
        target, at = SLOT[4], 15 + group
        if distance < 3:
            target, at = SLOT[sign * (distance + 1)], 5 * distance + group
        else:
            low, high = max(low, 4 * way), min(high, 4 * way + 4)
            if low >= high:
                return
        blocks = pl.ds(low, high - low)
        flights[2, color, way, distance + 1, group] = go(
            remote(
                buffers[color].at[SLOT[sign * distance], blocks],
                buffers[color].at[target, blocks],
                p2_send.at[color, way, at],
                p2_recv.at[color, way, at],
                "tm",
                second_axis[color](-sign),
            )
        )

    pairs = [(color, way) for way in (0, 1) for color in (0, 1)]

    def serve(event):
        stage, color, way, distance, group = event
        flights[event].wait_recv()
        if stage == 1:
            if distance < 4:
                send1(color, way, distance)
            if way == 1:
                for out_way in (0, 1):
                    send2(color, out_way, 0, distance)
        elif distance < 4:
            send2(color, way, distance, group)

    for color, way in pairs:
        send1(color, way, 0)
        send2(color, way, 0, 0)

    for copy in streams:
        copy.wait()
    grad_win[:rows] = (cotangent[...].astype(F32) * gates[...].astype(F32)).astype(BF16)
    rim_v = go(remote(values, value_rim, rim_send_sem.at[0], rim_recv_sem.at[0], "tm", after))
    rim_g = go(
        remote(
            grad_win.at[:rows], grad_win.at[rows:], rim_send_sem.at[1], rim_recv_sem.at[1], "tm", before
        )
    )

    def forward(first, data):
        cols = slice(0, rows) if first else slice(rows, 2 * rows)
        return mm(fwd_hi[:, cols], data) + mm(fwd_lo[:, cols], data)

    steps = {}
    for event in EVENTS:
        steps.setdefault(event[3] + event[4], []).append(event)

    for event in steps[1]:
        serve(event)
    for copy in ahead:
        copy.wait()
    spec_t[...] = forward(True, taps[...])
    spec_p[...] = forward(True, grad_win[:rows])
    spec_v[...] = forward(False, values[...])
    for event in steps[2]:
        serve(event)
    rim_v.wait_recv()
    has_before = (tm > 0).astype(F32)
    spec_v[...] = spec_v[...] + forward(True, value_rim[...]) * has_before
    rim_g.wait_recv()
    has_after = (tm < RING * RING - 1).astype(F32)
    spec_g[...] = spec_p[...] + forward(False, grad_win[rows:]) * has_after

    chans = values.shape[1]
    width = 128
    row_at = lax.broadcasted_iota(jnp.int32, (rows, width), 0)
    first_row = row_at == 0
    sign = (1 - 2 * (row_at & 1)).astype(F32)

    def product(left_re, left_im, right_re, right_im, flip):
        cross = left_im * right_im
        real = left_re * right_re
        if flip:
            imag = left_im * right_re - left_re * right_im
            real = real + jnp.where(first_row, 0.0, cross)
        else:
            imag = left_im * right_re + left_re * right_im
            real = real - jnp.where(first_row, 0.0, cross)
        return real, jnp.where(first_row, cross, imag)

    def keep(real, imag, at):
        for part, data in ((slice(0, rows), real), (slice(rows, 2 * rows), imag)):
            high = data.astype(BF16)
            prod_hi[part, at : at + width] = high
            prod_lo[part, at : at + width] = (data - high.astype(F32)).astype(BF16)

    for col in range(0, chans, width):
        cut = slice(col, col + width)
        v_re, v_im = spec_v[:rows, cut], spec_v[rows:, cut]
        t_re, t_im = spec_t[:rows, cut], spec_t[rows:, cut]
        g_re, g_im = spec_g[:rows, cut], spec_g[rows:, cut]
        p_re, p_im = spec_p[:rows, cut] * sign, spec_p[rows:, cut] * sign
        real, imag = product(v_re, v_im, t_re, t_im, False)
        keep(real * sign, imag * sign, col)
        real, imag = product(g_re, g_im, t_re, t_im, True)
        keep(real, imag, chans + col)
        real, imag = product(p_re, p_im, v_re, v_im, True)
        keep(real, imag, 2 * chans + col)

    def backward(index):
        cut = slice(index * chans, (index + 1) * chans)
        return (
            mm(inv_hi[...], prod_hi[:, cut])
            + mm(inv_hi[...], prod_lo[:, cut])
            + mm(inv_lo[...], prod_hi[:, cut])
        )

    def chain(own, send, got, send_sem, recv_sem, place, to):
        flying = {}

        def step(index):
            arrived = []
            for way, (length, sign) in enumerate(((3, 1), (4, -1))):
                if index > length:
                    continue
                if index:
                    flying[way, index - 1].wait_recv()
                    data = got[way, index - 1].astype(F32)
                if index == length:
                    flying[way] = data
                    continue
                mine = own[wrap(place + sign * (length - index))]
                if index:
                    mine = mine + data
                send[way, index] = mine.astype(send.dtype)
                flying[way, index] = go(
                    remote(
                        send.at[way, index],
                        got.at[way, index],
                        send_sem.at[way, index],
                        recv_sem.at[way, index],
                        "tm",
                        to(sign),
                    )
                )
            if index == 4:
                return own[place] + flying[0] + flying[1]

        return step

    for copy in later:
        copy.wait()
    lag_part[...] = (backward(2) * norm_scale).reshape(lag_part.shape)
    along_z = chain(lag_part, kz_send, kz_got, kz_send_sem, kz_recv_sem, z, at_z)
    along_y = chain(lag_row, ky_send, ky_got, ky_send_sem, ky_recv_sem, y, at_y)
    along_z(0)

    def chore(index):
        if index < 4:
            along_z(index)
        elif index == 4:
            total = along_z(4)
            lags = lag_row.shape[1]
            for at in range(RING):
                lag_row[at] = total[at * lags : (at + 1) * lags]
            along_y(0)
        elif index < 8:
            along_y(index - 4)
        else:
            kernel_grad[...] = along_y(4)

    left_v[...] = backward(1).T.astype(BF16)
    left_g[...] = (cotangent[...].astype(F32) * backward(0)).T.astype(BF16)

    parts = (part_a, part_b)
    pairs_got = (sib_a, sib_b)
    core = lax.rem(me, 2)
    chip = lax.div(me, 2)
    sibling = me + 1 - 2 * core

    def multiply(unit):
        color, slots, blocks = unit
        ref = buffers[color]
        shape = (slots[1] - slots[0], blocks[1] - blocks[0], 2, half // 2, rows)
        count = shape[0] * shape[1] * half
        cut = (slice(*slots), slice(*blocks))
        total = mm(ref[(*cut, 0)].reshape(count, chans), left_v[...])
        total = total + mm(ref[(*cut, 1)].reshape(count, chans), left_g[...])
        parts[color][cut] = total.astype(BF16).reshape(shape)
        at = (pl.ds(slots[0], shape[0]), pl.ds(blocks[0], shape[1]))
        index = UNITS.index(unit)
        return go(
            remote(
                parts[color].at[(*at, 1 - core)],
                pairs_got[color].at[at],
                sib_send.at[index],
                sib_recv.at[index],
                "chan",
                sibling,
            )
        )

    places = {slot: place for place, slot in SLOT.items()}

    def deliveries(unit):
        color, slots, blocks = unit
        group = GROUPS.index(slots)
        part = PARTS.index(blocks)
        found = []
        for slot in range(*(slots if color == 0 else blocks)):
            owner = wrap(z + places[slot])
            at = lax.rem(chip - lax.div(owner, 2) + 4, 4)
            if color == 0:
                lines = pl.ds(blocks[0], blocks[1] - blocks[0])
                src = part_a.at[slot, lines, core]
                dst = got_a.at[at, core, lines]
                sems = a_send.at[slot, part], a_recv.at[part, at, core]
            else:
                lines = pl.ds(slots[0], slots[1] - slots[0])
                src = part_b.at[lines, slot, core]
                dst = got_b.at[at, core, lines]
                sems = b_send.at[group, slot], b_recv.at[group, at, core]
            found.append((owner, src, dst, remote(src, dst, *sems, "chan", owner)))
        return found

    def finish(unit, flight):
        color, slots, blocks = unit
        flight.wait_recv()
        cut = (slice(*slots), slice(*blocks))
        total = parts[color][(*cut, core)].astype(F32) + pairs_got[color][cut].astype(F32)
        parts[color][(*cut, core)] = total.astype(BF16)
        for owner, src, dst, copy in deliveries(unit):

            @pl.when(owner != me)
            def _():
                copy.start()

            @pl.when(owner == me)
            def _():
                dst[...] = src[...]

    def needs(unit):
        color, slots, blocks = unit
        found = set()
        for slot in range(*slots):
            for block in range(*blocks):
                if slot == 0:
                    place = places[block]
                    ways = (0, 1) if place == 4 else (0,) if place < 0 else (1,)
                    if place:
                        found |= {(1, color, way, abs(place), 0) for way in ways}
                else:
                    way = (0 if block < 4 else 1) if slot == 7 else (0 if places[slot] < 0 else 1)
                    group = [low <= block < high for low, high in GROUPS].index(True)
                    found.add((2, color, way, abs(places[slot]), group))
        return found

    served = set(steps[1]) | set(steps[2])
    waiting = list(UNITS)
    pending = []

    def work():
        for unit in list(waiting):
            if needs(unit) <= served:
                waiting.remove(unit)
                pending.append((unit, multiply(unit)))
                if len(pending) > 1:
                    finish(*pending.pop(0))

    work()
    rest = [event for event in EVENTS if event not in served]
    for index, event in enumerate(rest):
        serve(event)
        served.add(event)
        work()
        if index + 1 in CHORES:
            chore(CHORES.index(index + 1) + 1)
    assert not waiting
    for unit, flight in pending:
        finish(unit, flight)

    for at in range(4):
        for which in (0, 1) if at else (1 - core,):
            for part, (low, high) in enumerate(PARTS):
                lines = pl.ds(low, high - low)
                remote(
                    part_a.at[0, lines, 0],
                    got_a.at[at, which, lines],
                    a_send.at[0, part],
                    a_recv.at[part, at, which],
                    "chan",
                    sibling,
                ).wait_recv()
            for group, (low, high) in enumerate(GROUPS):
                lines = pl.ds(low, high - low)
                remote(
                    part_b.at[lines, 0, 0],
                    got_b.at[at, which, lines],
                    b_send.at[group, 0],
                    b_recv.at[group, at, which],
                    "chan",
                    sibling,
                ).wait_recv()

    for pair in range(RING // 2):
        pieces = []
        for place in (2 * pair, 2 * pair + 1):
            block = slot_of(wrap(place - y))
            for got in (got_a, got_b):
                for which in (0, 1):
                    total = got[0, which, block].astype(F32)
                    for at in range(1, 4):
                        total = total + got[at, which, block].astype(F32)
                    pieces.append(total)
        merged = jnp.concatenate(pieces, 0)
        out[:, 4 * half * pair : 4 * half * (pair + 1)] = merged.T.astype(BF16)

    for copy in sends:
        copy.wait_send()
    for unit in UNITS:
        for owner, src, dst, copy in deliveries(unit):

            @pl.when(owner != me)
            def _():
                copy.wait_send()


def body(norm_scale, tables, *args):
    values, _, _, taps, value_weight, _ = args
    rows, chans = values.shape
    half = value_weight.shape[0] // 2
    lags = taps.shape[0] // (RING * RING)
    assert taps.shape[0] == rows and lax.axis_size("tm") == RING * RING
    assert lax.axis_size("chan") == RING and chans == RING * 2 * half
    vmem = pl.BlockSpec(memory_space=pltpu.VMEM)
    dma = pltpu.SemaphoreType.DMA
    done = pl.pallas_call(
        functools.partial(kernel, norm_scale),
        out_shape=(
            jax.ShapeDtypeStruct((rows, chans), BF16),
            jax.ShapeDtypeStruct((lags, chans), F32),
        ),
        in_specs=[pl.BlockSpec(memory_space=pl.ANY)] * 10,
        out_specs=(vmem, vmem),
        scratch_shapes=[
            pltpu.VMEM((rows, chans), BF16),
            pltpu.VMEM((rows, chans), BF16),
            pltpu.VMEM((rows, chans), BF16),
            pltpu.VMEM((rows, chans), BF16),
            *(pltpu.VMEM(table.shape, BF16) for table in tables),
            pltpu.VMEM((RING, RING, 2, half, chans), BF16),
            pltpu.VMEM((RING, RING, 2, half, chans), BF16),
            pltpu.VMEM((rows, chans), BF16),
            pltpu.VMEM((2 * rows, chans), BF16),
            pltpu.VMEM((2 * rows, chans), F32),
            pltpu.VMEM((2 * rows, chans), F32),
            pltpu.VMEM((2 * rows, chans), F32),
            pltpu.VMEM((2 * rows, chans), F32),
            pltpu.VMEM((2 * rows, 3 * chans), BF16),
            pltpu.VMEM((2 * rows, 3 * chans), BF16),
            pltpu.VMEM((chans, rows), BF16),
            pltpu.VMEM((chans, rows), BF16),
            pltpu.VMEM((RING, RING, 2, half // 2, rows), BF16),
            pltpu.VMEM((RING, RING, 2, half // 2, rows), BF16),
            pltpu.VMEM((RING, RING, half // 2, rows), BF16),
            pltpu.VMEM((RING, RING, half // 2, rows), BF16),
            pltpu.VMEM((4, 2, RING, half // 2, rows), BF16),
            pltpu.VMEM((4, 2, RING, half // 2, rows), BF16),
            pltpu.VMEM((RING, RING * lags, chans), F32),
            pltpu.VMEM((2, 4, RING * lags, chans), BF16),
            pltpu.VMEM((2, 4, RING * lags, chans), BF16),
            pltpu.VMEM((RING, lags, chans), F32),
            pltpu.VMEM((2, 4, lags, chans), F32),
            pltpu.VMEM((2, 4, lags, chans), F32),
            dma((12,)),
            dma((2,)),
            dma((2,)),
            dma((2, 2, 4)),
            dma((2, 2, 4)),
            dma((2, 2, 20)),
            dma((2, 2, 20)),
            dma((len(UNITS),)),
            dma((len(UNITS),)),
            dma((RING, len(PARTS))),
            dma((len(PARTS), 4, 2)),
            dma((len(GROUPS), RING)),
            dma((len(GROUPS), 4, 2)),
            dma((2, 4)),
            dma((2, 4)),
            dma((2, 4)),
            dma((2, 4)),
        ],
        compiler_params=pltpu.CompilerParams(
            collective_id=0, has_side_effects=True, vmem_limit_bytes=56 * 1024 * 1024
        ),
    )(*args, *tables)

    def hand_out(total, lags_in, out, lags_out):
        out[...] = total[...]
        lags_out[...] = lags_in[...]

    return pl.pallas_call(
        hand_out,
        out_shape=tuple(jax.ShapeDtypeStruct(array.shape, array.dtype) for array in done),
        in_specs=[vmem, vmem],
        out_specs=(vmem, vmem),
    )(*done)


def solution(mesh):
    placed = (
        P("tm", "chan"),
        P("tm", "chan"),
        P("tm", "chan"),
        P(None, "chan"),
        P("tm", "chan"),
        P("tm", "chan"),
    )

    def program(values, gates, cotangent, kernel_taps, value_weight, gate_weight):
        fwd, inv = dft_tables(kernel_taps.shape[0])
        tables = (*split_table(fwd), *split_table(inv))
        norm_scale = 1.0 / math.sqrt(values.shape[0])
        return jax.shard_map(
            lambda *args: body(norm_scale, args[6:], *args[:6]),
            mesh=mesh,
            in_specs=placed + (P(),) * 4,
            out_specs=(P("tm", "chan"), P("tm", "chan")),
            check_vma=False,
        )(values, gates, cotangent, kernel_taps, value_weight, gate_weight, *tables)

    return program
```
